768 devices in a mesh: seq: 48 (over z_lo, y, core), head: 16 (over z_hi, x).
Axes of the slice: x: 4, y: 8, z: 12 (z_hi: 4, z_lo: 3; z = z_hi * 3 + z_lo), core: 2. Of those that a mesh axis runs over, the one named last changes fastest.
Arguments:
- queries: bfloat16 [24576, 4096], P('seq', 'head'), may hold values from -16 to 16
- keys: bfloat16 [24576, 4096], P('seq', 'head'), may hold values from -16 to 16
- values: bfloat16 [24576, 4096], P('seq', 'head'), may hold values from -6 to 6
- segment_ids: int32 [24576], P('seq'), may hold values from 0 to 31, never falling along the last dimension, each value on 1 to 1024 neighbouring positions
- out_weight: bfloat16 [4096, 5120], P('head'), may hold values from -0.125 to 0.125
Outputs:
- mixed: bfloat16 [24576, 5120], P('seq', 'head')
The draws below stay inside these ranges and needn't reach their ends.
Inputs may be any that keep to these rules, and one draw needn't show every extreme that they name: `segment_ids`: segment numbers never fall along the sequence; a segment holds at most 1024 tokens.
All inputs are finite; a program needn't handle non-finite values.
Results may differ from the reference program's by a relative error of at most 0.02.
Values may be sent and summed in bfloat16 or wider, within the bound.
A program may use at most 64 MiB of HBM per device.

```python
import math
import jax
import jax.numpy as jnp
import numpy as np
from jax import lax

D = 5120
HD = 128
HEAD_DEV = 2
TOK_DEV = 512
SPAN = 2
HEADS = 32
TOKENS = 24576
SEG_MOST = 1024
N_SEQ = 48
N_HEAD = 16


def paired_draw(key):
    first, second = jax.random.split(jax.random.fold_in(key, 7), 2)
    shape = (TOKENS, HEADS * HD)
    query = jnp.clip(jax.random.normal(first, shape, jnp.float32), -6.0, 6.0)
    keyrow = jnp.clip(jax.random.normal(second, shape, jnp.float32), -6.0, 6.0)
    return (query, keyrow)


def draw_queries(key, part):
    return paired_draw(key)[0].astype(jnp.bfloat16)


def draw_keys(key, part):
    return paired_draw(key)[1].astype(jnp.bfloat16)


def with_spikes(values, key, source, target, shards_of, factor):
    owner, partner = [(jnp.arange(values.shape[axis_at]) // (values.shape[axis_at] // shards_of)).reshape([-1 if axis == axis_at else 1 for axis in range(values.ndim)]) for axis_at in (source, target)]
    chosen = jax.random.permutation(key, shards_of)[partner]
    strong = (owner == chosen) | (owner == (partner + shards_of // 2) % shards_of)
    return jnp.where(strong, factor * values, values)


def shard_levels(own_key, shape, cuts, low, top_value):
    factor_of = 1.0
    for dim, parts in cuts:
        draws = jax.random.uniform(jax.random.fold_in(jax.random.fold_in(own_key, 6), dim), (parts,), jnp.float32, low / len(cuts), top_value / len(cuts))
        factor_of = factor_of * jnp.repeat(jnp.exp(draws), shape[dim] // parts).reshape((-1,) + (1,) * (len(shape) - 1 - dim))
    return factor_of


def split_up(number_of, total, most, slope):
    loads = [(1 << 20) // math.isqrt(grade ** slope) + 1 for grade in range(2, number_of + 1)]
    surplus, holding = total - most - (number_of - 1), [1] * (number_of - 1)
    while surplus > 0:
        free = [i for i in range(number_of - 1) if holding[i] < most]
        mass, left = sum([loads[i] for i in free]), surplus
        for i in free:
            extra = min(most - holding[i], max(1, left * loads[i] // mass), surplus)
            holding[i] = holding[i] + extra
            surplus = surplus - extra
    return np.array([most] + holding)


def ragged_sizes(rng, count, total, bound, lean):
    if count == 2:
        one = jax.random.randint(rng, (), max(1, total - bound), min(bound, total - 1) + 1)
        return jnp.stack([one, total - one])
    tallies = jnp.asarray(split_up(count, total, bound, lean), jnp.int32)
    couples = (count - 1) // 2
    donor, sink = tallies[1:1 + 2 * couples:2], tallies[2:2 + 2 * couples:2]
    room = jnp.minimum(donor - 1, bound - sink)
    moved = jax.random.randint(jax.random.fold_in(rng, 1), (couples,), 0, 1 << 20) % (room + 1)
    tallies = tallies.at[1:1 + 2 * couples:2].set(donor - moved).at[2:2 + 2 * couples:2].set(sink + moved)
    return tallies[jax.random.permutation(jax.random.fold_in(rng, 2), count)]


def normal_values(stream_key, extent, scale, most, shards=(), held_as=jnp.bfloat16):
    result = scale * jax.random.normal(stream_key, extent, jnp.float32)
    if shards:
        result = result * shard_levels(stream_key, extent, shards, -0.22, 0.18)
    return jnp.clip(result, -most, most).astype(held_as)


def noise_with(key, extent, scale, most, cuts, heavy, held_as=jnp.bfloat16):
    entries = scale * jax.random.normal(key, extent, jnp.float32)
    if cuts:
        entries = entries * shard_levels(key, extent, cuts, -0.22, 0.18)
    return jnp.clip(with_spikes(entries, jax.random.fold_in(key, 3), *heavy), -most, most).astype(held_as)


def setup_inputs(seed: int = 0) -> dict:
    arg_keys = jax.random.split(jax.random.key(seed), 6)
    queries = draw_queries(jax.random.fold_in(arg_keys[5], 71), 0)
    keys = draw_keys(jax.random.fold_in(arg_keys[5], 71), 0)
    values = normal_values(arg_keys[2], (TOKENS, HEADS * HD), 1.0, 6.0, ((0, 48), (1, 16)))
    segment_ids = jnp.searchsorted(jnp.cumsum(ragged_sizes(arg_keys[3], 2 * N_SEQ // 3, TOKENS, SEG_MOST, 1)), jnp.arange(TOKENS), side="right").astype(jnp.int32)
    out_weight = noise_with(arg_keys[4], (HEADS * HD, D), (HEADS * HD) ** -0.5, 0.125, ((0, 16),), (0, 1, 16, 2.0))
    return {"queries": queries, "keys": keys, "values": values, "segment_ids": segment_ids, "out_weight": out_weight}


def reference(queries, keys, values, segment_ids, out_weight):
    width = HEADS * HD
    pad = SPAN * TOK_DEV
    keys_pad = jnp.concatenate([jnp.zeros((pad, width), keys.dtype), keys, jnp.zeros((pad, width), keys.dtype)], axis=0)
    values_pad = jnp.concatenate([jnp.zeros((pad, width), values.dtype), values, jnp.zeros((pad, width), values.dtype)], axis=0)
    neg = -jnp.ones((pad,), jnp.int32)
    seg_pad = jnp.concatenate([neg, segment_ids.astype(jnp.int32), neg], axis=0)
    window = (2 * SPAN + 1) * TOK_DEV

    def block(index):
        start = (index * TOK_DEV).astype(jnp.int32)
        query = lax.dynamic_slice_in_dim(queries, start, TOK_DEV, 0).astype(jnp.float32).reshape(TOK_DEV, HEADS, HD)
        qseg = lax.dynamic_slice_in_dim(segment_ids.astype(jnp.int32), start, TOK_DEV, 0)
        near_k = lax.dynamic_slice_in_dim(keys_pad, start, window, 0).astype(jnp.float32).reshape(window, HEADS, HD)
        near_v = lax.dynamic_slice_in_dim(values_pad, start, window, 0).astype(jnp.float32).reshape(window, HEADS, HD)
        kseg = lax.dynamic_slice_in_dim(seg_pad, start, window, 0)
        scores = jnp.einsum("qhd,khd->hqk", query, near_k) * (HD ** -0.5)
        allowed = (qseg[:, None] == kseg[None, :])[None]
        scores = jnp.where(allowed, scores, -1e30)
        peak = jnp.max(scores, axis=2)
        weights = jnp.where(allowed, jnp.exp(scores - peak[:, :, None]), 0.0)
        total = jnp.sum(weights, axis=2)
        rounded = lax.optimization_barrier(weights.astype(jnp.bfloat16)).astype(jnp.float32)
        summed = jnp.einsum("hqk,khd->qhd", rounded, near_v)
        attended = summed / jnp.transpose(total)[:, :, None]
        return attended.reshape(TOK_DEV, width).astype(jnp.bfloat16)

    attended = lax.map(block, jnp.arange(N_SEQ, dtype=jnp.int32)).reshape(TOKENS, width)
    group = HEAD_DEV * HD
    mixed = jnp.zeros((TOKENS, D), jnp.float32)
    for index in range(N_HEAD):
        term = jnp.dot(attended[:, index * group:(index + 1) * group], out_weight[index * group:(index + 1) * group], preferred_element_type=jnp.float32)
        mixed = mixed + term.astype(jnp.bfloat16).astype(jnp.float32)
    return mixed.astype(jnp.bfloat16)
```

```python
import functools
import math

import jax
import jax.numpy as jnp
from jax import lax
from jax.experimental import pallas as pl
from jax.experimental.pallas import tpu as pltpu
from jax.sharding import Mesh
from jax.sharding import PartitionSpec as P

Y = 8
ZH = 4
HD = 128
CH = 4
NEG = -1e30
MESH = pl.DeviceIdType.MESH
NEAR, FAR, PARTNER, RELAY, OWN = range(5)
IDS = 4


def tile_lanes(x, n):
    return jnp.concatenate([x] * n, axis=1)


def kernel(
    yn, xn, q_hbm, k_hbm, v_hbm, ids_hbm, w_hbm, out_ref,
    qv, kv, idr, qid, m_sc, l_sc, acc_sc, ag, wg, wrelay, xs, xr,
    kv_s, kv_r, wz_s, wz_r, wp_s, wp_r, wm_s, wm_r, wq_s, wq_r, az_s, az_r, x_s, x_r, loc,
):
    rows = q_hbm.shape[0]
    tr = rows // CH
    half = tr // 2
    slab = w_hbm.shape[2] // ZH
    own = out_ref.shape[1]
    win = xs.shape[3]
    factor = HD ** -0.5 * math.log2(math.e)

    s_at = lax.axis_index("seq")
    z_at = lax.axis_index("zh")
    x_at = lax.axis_index("x")
    sn = lax.axis_size("seq")
    core = lax.rem(s_at, 2)
    sgn = 2 * core - 1
    near = lax.rem(s_at + sgn + sn, sn)
    far_to = lax.rem(s_at - 2 * sgn + sn, sn)
    far_from = lax.rem(s_at + 2 * sgn + sn, sn)
    partner = s_at - sgn
    y_at = lax.rem(s_at // 2, yn)
    line = (s_at // (2 * yn)) * (2 * yn)
    y_up = line + lax.rem(y_at + 1, yn) * 2 + core
    y_down = line + lax.rem(y_at + yn - 1, yn) * 2 + core
    z_up = lax.rem(z_at + 1, ZH)
    z_two = lax.rem(z_at + 2, ZH)
    z_down = lax.rem(z_at + ZH - 1, ZH)

    def wblock(distance):
        return lax.rem(y_at + distance + 2 * yn, yn) * 2 + core

    me_block = 2 * y_at + core

    def remote(src, dst, send, recv, device):
        return pltpu.make_async_remote_copy(
            src_ref=src, dst_ref=dst, send_sem=send, recv_sem=recv,
            device_id=device, device_id_type=MESH,
        )

    sent = []

    def go(copy):
        copy.start()
        sent.append(copy)

    def piece_src(p):
        if p == IDS:
            return ids_hbm
        src = k_hbm if p % 2 == 0 else v_hbm
        return src.at[:, pl.ds((p // 2) * HD, HD)]

    def piece_dst(p, slot):
        return idr.at[slot] if p == IDS else kv.at[slot, p]

    targets = {NEAR: {"seq": near}, FAR: {"seq": far_to}, PARTNER: {"seq": partner}, RELAY: {"seq": partner}}

    def piece(p, slot):
        src = piece_dst(p, NEAR) if slot == RELAY else piece_src(p)
        return remote(src, piece_dst(p, slot), kv_s.at[p, slot], kv_r.at[p, slot], targets[slot])

    def cols(z):
        return pl.ds(pl.multiple_of(z * slab, 128), slab)

    local = [pltpu.make_async_copy(piece_src(p), piece_dst(p, OWN), loc.at[p]) for p in range(5)]
    local.append(pltpu.make_async_copy(q_hbm, qv, loc.at[5]))
    w_local = pltpu.make_async_copy(w_hbm.at[:, :, cols(z_at)], wg.at[:, 0], loc.at[6])
    for copy in local:
        copy.start()
    w_local.start()

    barrier = pltpu.get_barrier_semaphore()
    peers = [{"seq": near}, {"seq": partner}, {"seq": far_to}, {"seq": far_from}, {"seq": y_up}, {"seq": y_down},
             {"zh": z_up}, {"zh": z_down}]
    peers += [{"x": lax.rem(x_at + r, xn)} for r in range(1, xn)]
    for peer in peers:
        pl.semaphore_signal(barrier, inc=1, device_id=peer, device_id_type=MESH)
    pl.semaphore_wait(barrier, len(peers))

    for p in (IDS, 0, 1):
        for slot in (NEAR, FAR, PARTNER):
            go(piece(p, slot))
    wz = [
        remote(w_hbm.at[me_block, :, cols(z_two)], wrelay, wz_s.at[0], wz_r.at[0], {"zh": z_up}),
        remote(w_hbm.at[me_block, :, cols(z_up)], wg.at[me_block, 1], wz_s.at[1], wz_r.at[1], {"zh": z_up}),
        remote(w_hbm.at[me_block, :, cols(z_down)], wg.at[me_block, 3], wz_s.at[2], wz_r.at[2], {"zh": z_down}),
        remote(wrelay, wg.at[me_block, 2], wz_s.at[3], wz_r.at[3], {"zh": z_up}),
    ]
    for copy in wz[:3]:
        go(copy)
    for p in (2, 3):
        for slot in (NEAR, FAR, PARTNER):
            go(piece(p, slot))

    for copy in local:
        copy.wait()
    for i in range(rows // 128):
        wide = jnp.broadcast_to(idr[OWN, 0:1, i * 128:(i + 1) * 128].astype(jnp.float32), (128, 128))
        qid[i * 128:(i + 1) * 128, :] = jnp.transpose(wide)

    def attn(slot, head, first=False):
        def body(t, carry):
            at = pl.ds(pl.multiple_of(t * tr, tr), tr)
            q = qv[at, head * HD:(head + 1) * HD]
            scores = lax.dot_general(
                q, kv[slot, 2 * head], (((1,), (1,)), ((), ())), preferred_element_type=jnp.float32
            )
            n = rows // HD
            mine = tile_lanes(qid[at, :], n)
            theirs = jnp.broadcast_to(idr[slot, 0:1, :].astype(jnp.float32), (tr, rows))
            scores = jnp.where(mine == theirs, scores, NEG)
            top = jnp.broadcast_to(jnp.max(scores, axis=1, keepdims=True), (tr, HD))
            if not first:
                old = m_sc[at, :]
                top = jnp.maximum(old, top)
            weights = jnp.exp2((scores - tile_lanes(top, n)) * factor)
            part = weights[:, :HD]
            for i in range(1, n):
                part = part + weights[:, i * HD:(i + 1) * HD]
            summed = jnp.dot(weights.astype(jnp.bfloat16), kv[slot, 2 * head + 1], preferred_element_type=jnp.float32)
            if not first:
                scale = jnp.exp2((old - top) * factor)
                part = part + l_sc[at, :] * scale
                summed = summed + acc_sc[at, :] * scale
            m_sc[at, :] = top
            l_sc[at, :] = part
            acc_sc[at, :] = summed
            return carry

        lax.fori_loop(0, CH, body, 0)

    def finish(head, chunk):
        at = pl.ds(chunk * tr, tr)
        total = jnp.sum(l_sc[at, :], axis=1, keepdims=True)
        ag[0, head, at, :] = (acc_sc[at, :] / total).astype(jnp.bfloat16)

    def az(head, chunk, kind):
        at = pl.ds(chunk * tr, tr)
        low, high = pl.ds(chunk * tr, half), pl.ds(chunk * tr + half, half)
        src, dst, to = [
            (ag.at[0, head, at], ag.at[1, head, at], z_up),
            (ag.at[0, head, at], ag.at[3, head, at], z_down),
            (ag.at[1, head, low], ag.at[2, head, low], z_up),
            (ag.at[3, head, high], ag.at[2, head, high], z_down),
        ][kind]
        return remote(src, dst, az_s.at[head, chunk, kind], az_r.at[head, chunk, kind], {"zh": to})

    def z_relay(head, chunk):
        for kind in (0, 1):
            az(head, chunk, kind).wait_recv()
            go(az(head, chunk, kind + 2))

    ups, downs = yn // 2, (yn - 1) // 2

    def w_step(kind, t):
        if kind == "up":
            src, sems, to = wblock(-t), (wp_s.at[t], wp_r.at[t]), y_up
        elif kind == "down":
            src, sems, to = wblock(t), (wm_s.at[t], wm_r.at[t]), y_down
        else:
            src, sems, to = wblock(t), (wq_s.at[t % yn], wq_r.at[t % yn]), partner
        block = wg.at[src, pl.ds(1, ZH - 1)]
        return remote(block, block, *sems, {"seq": to})

    def w_advance(t):
        w_step("up", t).wait_recv()
        if t + 1 < ups:
            go(w_step("up", t + 1))
        go(w_step("partner", -1 - t))
        if t < downs:
            w_step("down", t).wait_recv()
            if t + 1 < downs:
                go(w_step("down", t + 1))
            go(w_step("partner", 1 + t))

    def arrive(slot, *pieces):
        for p in pieces:
            piece(p, slot).wait_recv()
            if slot == NEAR:
                go(piece(p, RELAY))

    attn(OWN, 0, first=True)
    arrive(PARTNER, IDS, 0, 1)
    attn(PARTNER, 0)
    arrive(NEAR, IDS, 0, 1)
    attn(NEAR, 0)
    wz[0].wait_recv()
    go(wz[3])
    arrive(FAR, IDS, 0, 1)
    attn(FAR, 0)
    arrive(RELAY, IDS, 0, 1)
    attn(RELAY, 0)
    for c in range(CH):
        finish(0, c)
        go(az(0, c, 0))
        go(az(0, c, 1))

    arrive(NEAR, 2, 3)
    attn(OWN, 1, first=True)
    for copy in wz[1:]:
        copy.wait_recv()
    go(w_step("up", 0))
    go(w_step("down", 0))
    go(w_step("partner", 0))
    arrive(PARTNER, 2, 3)
    attn(PARTNER, 1)
    attn(NEAR, 1)
    z_relay(0, 0)
    arrive(FAR, 2, 3)
    attn(FAR, 1)
    z_relay(0, 1)
    arrive(RELAY, 2, 3)
    attn(RELAY, 1)
    for c in range(CH):
        finish(1, c)
        go(az(1, c, 0))
        go(az(1, c, 1))
        if c == 1:
            z_relay(0, 2)
        if c == 2:
            z_relay(0, 3)
    for t in range(max(ups, CH)):
        if t < ups:
            w_advance(t)
        if t < CH:
            z_relay(1, t)
    w_local.wait()
    for t in range(yn):
        w_step("partner", t).wait_recv()

    def project(c):
        at = pl.ds(c * tr, tr)
        for head in range(2):
            for kind in (2, 3):
                az(head, c, kind).wait_recv()
        total = None
        for head in range(2):
            left = jnp.concatenate([ag[r, head, at, :] for r in range(ZH)], axis=1)
            n = wg.shape[0] // 2
            right = jnp.concatenate(
                [wg[head * n:(head + 1) * n, r].reshape(HD, slab) for r in range(ZH)], axis=0
            )
            term = jnp.dot(left, right, preferred_element_type=jnp.float32)
            total = term if total is None else total + term
        total = total.astype(jnp.bfloat16)
        for x in range(xn):
            start = (x * own // HD) * HD
            xs[c, x] = total[:, start:start + win]

    def x_copy(c, r):
        to = lax.rem(x_at + r, xn)
        return remote(xs.at[c, to], xr.at[c, r - 1], x_s.at[c, r - 1], x_r.at[c, r - 1], {"x": to})

    for c in range(CH):
        project(c)
        for r in range(1, xn):
            go(x_copy(c, r))

    odd = lax.rem(x_at, 2) == 1
    for c in range(CH):
        total = xs[c, x_at].astype(jnp.float32)
        for r in range(1, xn):
            x_copy(c, r).wait_recv()
            total = total + xr[c, r - 1].astype(jnp.float32)
        mixed = jnp.where(odd, total[:, win - own:], total[:, :own])
        out_ref[c * tr:(c + 1) * tr, :] = mixed.astype(jnp.bfloat16)
    for copy in sent:
        copy.wait_send()


def shards(yn, xn, queries, keys, values, segment_ids, out_weight):
    rows = queries.shape[0]
    depth, features = out_weight.shape
    own = features // (ZH * xn)
    win = -(-own // HD) * HD
    slab = features // ZH
    wb = depth // (2 * yn)
    ids = jnp.broadcast_to(segment_ids[None, :], (8, rows))
    weight = out_weight.reshape(2 * yn, wb, features)
    dma = pltpu.SemaphoreType.DMA
    bf16, f32 = jnp.bfloat16, jnp.float32
    hbm = pl.BlockSpec(memory_space=pl.ANY)
    ups, downs = yn // 2, max(1, (yn - 1) // 2)
    return pl.pallas_call(
        functools.partial(kernel, yn, xn),
        out_shape=jax.ShapeDtypeStruct((rows, own), bf16),
        in_specs=[hbm] * 5,
        out_specs=pl.BlockSpec(memory_space=pltpu.VMEM),
        scratch_shapes=[
            pltpu.VMEM((rows, 2 * HD), bf16),
            pltpu.VMEM((5, 4, rows, HD), bf16),
            pltpu.VMEM((5, 8, rows), jnp.int32),
            pltpu.VMEM((rows, HD), f32),
            pltpu.VMEM((rows, HD), f32),
            pltpu.VMEM((rows, HD), f32),
            pltpu.VMEM((rows, HD), f32),
            pltpu.VMEM((ZH, 2, rows, HD), bf16),
            pltpu.VMEM((2 * yn, ZH, wb, slab), bf16),
            pltpu.VMEM((wb, slab), bf16),
            pltpu.VMEM((CH, xn, rows // CH, win), bf16),
            pltpu.VMEM((CH, xn - 1, rows // CH, win), bf16),
            dma((5, 4)), dma((5, 4)),
            dma((4,)), dma((4,)),
            dma((ups,)), dma((ups,)),
            dma((downs,)), dma((downs,)),
            dma((yn,)), dma((yn,)),
            dma((2, CH, 4)), dma((2, CH, 4)),
            dma((CH, xn - 1)), dma((CH, xn - 1)),
            dma((7,)),
        ],
        compiler_params=pltpu.CompilerParams(
            collective_id=0, has_side_effects=True, vmem_limit_bytes=60 * 1024 * 1024
        ),
    )(queries, keys, values, ids, weight)


def build(mesh, yn):
    sn, hn = mesh.shape["seq"], mesh.shape["head"]
    torus = Mesh(mesh.devices.reshape(sn, ZH, hn // ZH), ("seq", "zh", "x"))
    head = ("zh", "x")
    in_specs = (P("seq", head), P("seq", head), P("seq", head), P("seq"), P(head, None))
    return jax.shard_map(
        functools.partial(shards, yn, hn // ZH),
        mesh=torus, in_specs=in_specs, out_specs=P("seq", head), check_vma=False,
    )


def solution(mesh):
    return build(mesh, Y)
```

```python
import functools
import math

import jax
import jax.numpy as jnp
from jax import lax
from jax.experimental import pallas as pl
from jax.experimental.pallas import tpu as pltpu
from jax.sharding import Mesh
from jax.sharding import PartitionSpec as P

Y = 8
ZH = 4
HD = 128
CH = 4
NEG = -1e30
MESH = pl.DeviceIdType.MESH
NEAR, FAR, PARTNER, RELAY, OWN = range(5)
IDS = 4


def tile_lanes(x, n):
    return jnp.concatenate([x] * n, axis=1)


def kernel(
    yn, xn, q_hbm, k_hbm, v_hbm, ids_hbm, w_hbm, out_hbm,
    qv, kv, idr, qid, m_sc, l_sc, acc_sc, ag, wg, wrelay, xs, xr, ot,
    kv_s, kv_r, wz_s, wz_r, wp_s, wp_r, wm_s, wm_r, wq_s, wq_r, az_s, az_r, x_s, x_r, o_s, loc,
):
    rows = q_hbm.shape[0]
    tr = rows // CH
    half = tr // 2
    slab = w_hbm.shape[2] // ZH
    own = out_hbm.shape[0]
    win = xs.shape[3]
    factor = HD ** -0.5 * math.log2(math.e)

    s_at = lax.axis_index("seq")
    z_at = lax.axis_index("zh")
    x_at = lax.axis_index("x")
    sn = lax.axis_size("seq")
    core = lax.rem(s_at, 2)
    sgn = 2 * core - 1
    near = lax.rem(s_at + sgn + sn, sn)
    far_to = lax.rem(s_at - 2 * sgn + sn, sn)
    far_from = lax.rem(s_at + 2 * sgn + sn, sn)
    partner = s_at - sgn
    y_at = lax.rem(s_at // 2, yn)
    line = (s_at // (2 * yn)) * (2 * yn)
    y_up = line + lax.rem(y_at + 1, yn) * 2 + core
    y_down = line + lax.rem(y_at + yn - 1, yn) * 2 + core
    z_up = lax.rem(z_at + 1, ZH)
    z_two = lax.rem(z_at + 2, ZH)
    z_down = lax.rem(z_at + ZH - 1, ZH)

    def wblock(distance):
        return lax.rem(y_at + distance + 2 * yn, yn) * 2 + core

    me_block = 2 * y_at + core

    def remote(src, dst, send, recv, device):
        return pltpu.make_async_remote_copy(
            src_ref=src, dst_ref=dst, send_sem=send, recv_sem=recv,
            device_id=device, device_id_type=MESH,
        )

    sent = []

    def go(copy):
        copy.start()
        sent.append(copy)

    def piece_src(p):
        if p == IDS:
            return ids_hbm
        src = k_hbm if p % 2 == 0 else v_hbm
        return src.at[:, pl.ds((p // 2) * HD, HD)]

    def piece_dst(p, slot):
        return idr.at[slot] if p == IDS else kv.at[slot, p]

    targets = {NEAR: {"seq": near}, FAR: {"seq": far_to}, PARTNER: {"seq": partner}, RELAY: {"seq": partner}}

    def piece(p, slot):
        src = piece_dst(p, NEAR) if slot == RELAY else piece_src(p)
        return remote(src, piece_dst(p, slot), kv_s.at[p, slot], kv_r.at[p, slot], targets[slot])

    def cols(z):
        return pl.ds(pl.multiple_of(z * slab, 128), slab)

    local = [pltpu.make_async_copy(piece_src(p), piece_dst(p, OWN), loc.at[p]) for p in range(5)]
    local.append(pltpu.make_async_copy(q_hbm, qv, loc.at[5]))
    w_local = pltpu.make_async_copy(w_hbm.at[:, :, cols(z_at)], wg.at[:, 0], loc.at[6])
    for copy in local:
        copy.start()
    w_local.start()

    barrier = pltpu.get_barrier_semaphore()
    peers = [{"seq": near}, {"seq": partner}, {"seq": far_to}, {"seq": far_from}, {"seq": y_up}, {"seq": y_down},
             {"zh": z_up}, {"zh": z_down}]
    peers += [{"x": lax.rem(x_at + r, xn)} for r in range(1, xn)]
    for peer in peers:
        pl.semaphore_signal(barrier, inc=1, device_id=peer, device_id_type=MESH)
    pl.semaphore_wait(barrier, len(peers))

    for p in (IDS, 0, 1):
        for slot in (NEAR, FAR, PARTNER):
            go(piece(p, slot))
    wz = [
        remote(w_hbm.at[me_block, :, cols(z_two)], wrelay, wz_s.at[0], wz_r.at[0], {"zh": z_up}),
        remote(w_hbm.at[me_block, :, cols(z_up)], wg.at[me_block, 1], wz_s.at[1], wz_r.at[1], {"zh": z_up}),
        remote(w_hbm.at[me_block, :, cols(z_down)], wg.at[me_block, 3], wz_s.at[2], wz_r.at[2], {"zh": z_down}),
        remote(wrelay, wg.at[me_block, 2], wz_s.at[3], wz_r.at[3], {"zh": z_up}),
    ]
    for copy in wz[:3]:
        go(copy)
    for p in (2, 3):
        for slot in (NEAR, FAR, PARTNER):
            go(piece(p, slot))

    for copy in local:
        copy.wait()
    for i in range(rows // 128):
        wide = jnp.broadcast_to(idr[OWN, 0:1, i * 128:(i + 1) * 128].astype(jnp.float32), (128, 128))
        qid[i * 128:(i + 1) * 128, :] = jnp.transpose(wide)

    def attn(slot, head, first=False):
        def body(t, carry):
            at = pl.ds(pl.multiple_of(t * tr, tr), tr)
            q = qv[at, head * HD:(head + 1) * HD]
            scores = lax.dot_general(
                q, kv[slot, 2 * head], (((1,), (1,)), ((), ())), preferred_element_type=jnp.float32
            )
            n = rows // HD
            mine = tile_lanes(qid[at, :], n)
            theirs = jnp.broadcast_to(idr[slot, 0:1, :].astype(jnp.float32), (tr, rows))
            scores = jnp.where(mine == theirs, scores, NEG)
            top = jnp.broadcast_to(jnp.max(scores, axis=1, keepdims=True), (tr, HD))
            if not first:
                old = m_sc[at, :]
                top = jnp.maximum(old, top)
            weights = jnp.exp2((scores - tile_lanes(top, n)) * factor)
            part = weights[:, :HD]
            for i in range(1, n):
                part = part + weights[:, i * HD:(i + 1) * HD]
            summed = jnp.dot(weights.astype(jnp.bfloat16), kv[slot, 2 * head + 1], preferred_element_type=jnp.float32)
            if not first:
                scale = jnp.exp2((old - top) * factor)
                part = part + l_sc[at, :] * scale
                summed = summed + acc_sc[at, :] * scale
            m_sc[at, :] = top
            l_sc[at, :] = part
            acc_sc[at, :] = summed
            return carry

        lax.fori_loop(0, CH, body, 0, unroll=True)

    def finish(head, chunk):
        at = pl.ds(chunk * tr, tr)
        total = jnp.sum(l_sc[at, :], axis=1, keepdims=True)
        ag[0, head, at, :] = (acc_sc[at, :] / total).astype(jnp.bfloat16)

    def az(head, chunk, kind):
        at = pl.ds(chunk * tr, tr)
        low, high = pl.ds(chunk * tr, half), pl.ds(chunk * tr + half, half)
        src, dst, to = [
            (ag.at[0, head, at], ag.at[1, head, at], z_up),
            (ag.at[0, head, at], ag.at[3, head, at], z_down),
            (ag.at[1, head, low], ag.at[2, head, low], z_up),
            (ag.at[3, head, high], ag.at[2, head, high], z_down),
        ][kind]
        return remote(src, dst, az_s.at[head, chunk, kind], az_r.at[head, chunk, kind], {"zh": to})

    def z_relay(head, chunk):
        for kind in (0, 1):
            az(head, chunk, kind).wait_recv()
            go(az(head, chunk, kind + 2))

    def z_direct(head, chunk):
        go(az(head, chunk, 0))
        go(az(head, chunk, 1))

    ups, downs = yn // 2, (yn - 1) // 2

    def w_step(kind, t):
        if kind == "up":
            src, sems, to = wblock(-t), (wp_s.at[t], wp_r.at[t]), y_up
        elif kind == "down":
            src, sems, to = wblock(t), (wm_s.at[t], wm_r.at[t]), y_down
        else:
            src, sems, to = wblock(t), (wq_s.at[t % yn], wq_r.at[t % yn]), partner
        block = wg.at[src, pl.ds(1, ZH - 1)]
        return remote(block, block, *sems, {"seq": to})

    def w_advance(t):
        if t >= ups:
            return
        w_step("up", t).wait_recv()
        if t + 1 < ups:
            go(w_step("up", t + 1))
        go(w_step("partner", -1 - t))
        if t < downs:
            w_step("down", t).wait_recv()
            if t + 1 < downs:
                go(w_step("down", t + 1))
            go(w_step("partner", 1 + t))

    def arrive(slot, *pieces):
        for p in pieces:
            piece(p, slot).wait_recv()
            if slot == NEAR:
                go(piece(p, RELAY))

    attn(OWN, 0, first=True)
    arrive(PARTNER, IDS, 0, 1)
    attn(PARTNER, 0)
    wz[0].wait_recv()
    go(wz[3])
    arrive(NEAR, IDS, 0, 1)
    attn(NEAR, 0)
    arrive(FAR, IDS, 0, 1)
    attn(FAR, 0)
    arrive(RELAY, IDS, 0, 1)
    attn(RELAY, 0)
    for c in range(CH):
        finish(0, c)
        z_direct(0, c)

    for copy in wz[1:]:
        copy.wait_recv()
    go(w_step("up", 0))
    go(w_step("down", 0))
    go(w_step("partner", 0))
    arrive(NEAR, 2, 3)
    attn(OWN, 1, first=True)
    arrive(PARTNER, 2, 3)
    attn(PARTNER, 1)
    z_relay(0, 0)
    attn(NEAR, 1)
    z_relay(0, 1)
    arrive(FAR, 2, 3)
    attn(FAR, 1)
    w_advance(0)
    arrive(RELAY, 2, 3)
    attn(RELAY, 1)
    for c in range(CH):
        finish(1, c)
        if c < 2:
            z_direct(1, c)
    z_relay(0, 2)
    w_advance(1)
    z_relay(0, 3)
    for t in range(2, max(ups, 4)):
        w_advance(t)
        z_relay(1, t - 2)
        z_direct(1, t)
    w_local.wait()
    for t in range(yn):
        w_step("partner", t).wait_recv()

    def project(c):
        at = pl.ds(c * tr, tr)
        for head in range(2):
            for kind in (2, 3):
                az(head, c, kind).wait_recv()
        total = None
        for head in range(2):
            left = jnp.concatenate([ag[r, head, at, :] for r in range(ZH)], axis=1)
            n = wg.shape[0] // 2
            right = jnp.concatenate(
                [wg[head * n:(head + 1) * n, r].reshape(HD, slab) for r in range(ZH)], axis=0
            )
            term = jnp.dot(left, right, preferred_element_type=jnp.float32)
            total = term if total is None else total + term
        total = total.astype(jnp.bfloat16)
        for x in range(xn):
            start = (x * own // HD) * HD
            xs[c, x] = total[:, start:start + win]
        for r in range(1, xn):
            go(x_copy(c, r))

    def x_copy(c, r):
        to = lax.rem(x_at + r, xn)
        return remote(xs.at[c, to], xr.at[c, r - 1], x_s.at[c, r - 1], x_r.at[c, r - 1], {"x": to})

    odd = lax.rem(x_at, 2) == 1

    def out_copy(c):
        return pltpu.make_async_copy(ot.at[c], out_hbm.at[:, pl.ds(c * tr, tr)], o_s.at[c])

    def mix(c):
        total = xs[c, x_at].astype(jnp.float32)
        for r in range(1, xn):
            x_copy(c, r).wait_recv()
            total = total + xr[c, r - 1].astype(jnp.float32)
        total = jnp.transpose(total)
        mixed = jnp.where(odd, total[win - own:], total[:own])
        ot[c] = mixed.astype(jnp.bfloat16)
        out_copy(c).start()

    project(0)
    z_relay(1, 2)
    project(1)
    z_relay(1, 3)
    mix(0)
    project(2)
    mix(1)
    project(3)
    mix(2)
    mix(3)
    for copy in sent:
        copy.wait_send()
    for c in range(CH):
        out_copy(c).wait()


def shards(yn, xn, queries, keys, values, segment_ids, out_weight):
    rows = queries.shape[0]
    depth, features = out_weight.shape
    own = features // (ZH * xn)
    win = -(-own // HD) * HD
    slab = features // ZH
    wb = depth // (2 * yn)
    ids = segment_ids.reshape(1, rows)
    weight = out_weight.reshape(2 * yn, wb, features)
    dma = pltpu.SemaphoreType.DMA
    bf16, f32 = jnp.bfloat16, jnp.float32
    hbm = pl.BlockSpec(memory_space=pl.ANY)
    ups, downs = yn // 2, max(1, (yn - 1) // 2)
    out = pl.pallas_call(
        functools.partial(kernel, yn, xn),
        out_shape=jax.ShapeDtypeStruct((own, rows), bf16),
        in_specs=[hbm] * 5,
        out_specs=hbm,
        scratch_shapes=[
            pltpu.VMEM((rows, 2 * HD), bf16),
            pltpu.VMEM((5, 4, rows, HD), bf16),
            pltpu.VMEM((5, 1, rows), jnp.int32),
            pltpu.VMEM((rows, HD), f32),
            pltpu.VMEM((rows, HD), f32),
            pltpu.VMEM((rows, HD), f32),
            pltpu.VMEM((rows, HD), f32),
            pltpu.VMEM((ZH, 2, rows, HD), bf16),
            pltpu.VMEM((2 * yn, ZH, wb, slab), bf16),
            pltpu.VMEM((wb, slab), bf16),
            pltpu.VMEM((CH, xn, rows // CH, win), bf16),
            pltpu.VMEM((CH, xn - 1, rows // CH, win), bf16),
            pltpu.VMEM((CH, own, rows // CH), bf16),
            dma((5, 4)), dma((5, 4)),
            dma((4,)), dma((4,)),
            dma((ups,)), dma((ups,)),
            dma((downs,)), dma((downs,)),
            dma((yn,)), dma((yn,)),
            dma((2, CH, 4)), dma((2, CH, 4)),
            dma((CH, xn - 1)), dma((CH, xn - 1)),
            dma((CH,)), dma((7,)),
        ],
        compiler_params=pltpu.CompilerParams(
            collective_id=0, has_side_effects=True, vmem_limit_bytes=60 * 1024 * 1024
        ),
    )(queries, keys, values, ids, weight)
    return jnp.transpose(out)


def build(mesh, yn):
    sn, hn = mesh.shape["seq"], mesh.shape["head"]
    torus = Mesh(mesh.devices.reshape(sn, ZH, hn // ZH), ("seq", "zh", "x"))
    head = ("zh", "x")
    in_specs = (P("seq", head), P("seq", head), P("seq", head), P("seq"), P(head, None))
    return jax.shard_map(
        functools.partial(shards, yn, hn // ZH),
        mesh=torus, in_specs=in_specs, out_specs=P("seq", head), check_vma=False,
    )


def solution(mesh):
    return build(mesh, Y)
```

```python
import functools
import math

import jax
import jax.numpy as jnp
from jax import lax
from jax.experimental import pallas as pl
from jax.experimental.pallas import tpu as pltpu
from jax.sharding import Mesh
from jax.sharding import PartitionSpec as P

Y = 8
ZH = 4
HD = 128
CH = 4
NEG = -1e30
MESH = pl.DeviceIdType.MESH
NEAR, FAR, PARTNER, RELAY, OWN = range(5)
IDS = 4


def tile_lanes(x, n):
    return jnp.concatenate([x] * n, axis=1)


def kernel(
    yn, xn, q_hbm, k_hbm, v_hbm, ids_hbm, w_hbm, out_hbm,
    qv, kv, idr, qid, m_sc, l_sc, acc_sc, ag, wg, wrelay, xs, xr, ot,
    kv_s, kv_r, wz_s, wz_r, wp_s, wp_r, wm_s, wm_r, wq_s, wq_r, az_s, az_r, x_s, x_r, o_s, loc,
):
    rows = q_hbm.shape[0]
    tr = rows // CH
    slab = w_hbm.shape[2] // ZH
    own = out_hbm.shape[0]
    factor = HD ** -0.5 * math.log2(math.e)

    s_at = lax.axis_index("seq")
    z_at = lax.axis_index("zh")
    x_at = lax.axis_index("x")
    sn = lax.axis_size("seq")
    core = lax.rem(s_at, 2)
    sgn = 2 * core - 1
    near = lax.rem(s_at + sgn + sn, sn)
    far_to = lax.rem(s_at - 2 * sgn + sn, sn)
    far_from = lax.rem(s_at + 2 * sgn + sn, sn)
    partner = s_at - sgn
    y_at = lax.rem(s_at // 2, yn)
    line = (s_at // (2 * yn)) * (2 * yn)
    y_up = line + lax.rem(y_at + 1, yn) * 2 + core
    y_down = line + lax.rem(y_at + yn - 1, yn) * 2 + core
    z_up = lax.rem(z_at + 1, ZH)
    z_two = lax.rem(z_at + 2, ZH)
    z_down = lax.rem(z_at + ZH - 1, ZH)

    def wblock(distance):
        return lax.rem(y_at + distance + 2 * yn, yn) * 2 + core

    me_block = 2 * y_at + core

    def remote(src, dst, send, recv, device):
        return pltpu.make_async_remote_copy(
            src_ref=src, dst_ref=dst, send_sem=send, recv_sem=recv,
            device_id=device, device_id_type=MESH,
        )

    sent = []

    outer = jnp.logical_and(s_at + sgn >= 0, s_at + sgn < sn)
    inner = jnp.logical_and(s_at - 2 * sgn >= 0, s_at - 2 * sgn < sn)

    def where(condition, act):
        if condition is None:
            act()
        else:
            pl.when(condition)(act)

    def go(copy, condition=None):
        where(condition, copy.start)
        sent.append((copy, condition))

    def piece_src(p):
        if p == IDS:
            return ids_hbm
        src = k_hbm if p % 2 == 0 else v_hbm
        return src.at[:, pl.ds((p // 2) * HD, HD)]

    def piece_dst(p, slot):
        return idr.at[slot] if p == IDS else kv.at[slot, p]

    targets = {NEAR: {"seq": near}, FAR: {"seq": far_to}, PARTNER: {"seq": partner}, RELAY: {"seq": partner}}

    gives = {NEAR: outer, FAR: inner, PARTNER: None, RELAY: outer}
    gets = {NEAR: outer, FAR: outer, PARTNER: None, RELAY: inner, OWN: None}

    def piece(p, slot):
        src = piece_dst(p, NEAR) if slot == RELAY else piece_src(p)
        return remote(src, piece_dst(p, slot), kv_s.at[p, slot], kv_r.at[p, slot], targets[slot])

    def cols(z):
        return pl.ds(pl.multiple_of(z * slab, 128), slab)

    local = [pltpu.make_async_copy(piece_src(p), piece_dst(p, OWN), loc.at[p]) for p in range(5)]
    local.append(pltpu.make_async_copy(q_hbm, qv, loc.at[5]))
    w_local = pltpu.make_async_copy(w_hbm.at[:, :, cols(z_at)], wg.at[:, 0], loc.at[6])
    for copy in local:
        copy.start()
    w_local.start()

    barrier = pltpu.get_barrier_semaphore()
    peers = [{"seq": near}, {"seq": partner}, {"seq": far_to}, {"seq": far_from}, {"seq": y_up}, {"seq": y_down},
             {"zh": z_up}, {"zh": z_down}]
    peers += [{"x": lax.rem(x_at + r, xn)} for r in range(1, xn)]
    for peer in peers:
        pl.semaphore_signal(barrier, inc=1, device_id=peer, device_id_type=MESH)
    pl.semaphore_wait(barrier, len(peers))

    by = jnp.where(core == 0, z_up, z_down)
    wz = [
        remote(w_hbm.at[me_block, :, cols(z_two)], wrelay, wz_s.at[0], wz_r.at[0], {"zh": by}),
        remote(w_hbm.at[me_block, :, cols(z_up)], wg.at[me_block, 1], wz_s.at[1], wz_r.at[1], {"zh": z_up}),
        remote(w_hbm.at[me_block, :, cols(z_down)], wg.at[me_block, 3], wz_s.at[2], wz_r.at[2], {"zh": z_down}),
        remote(wrelay, wg.at[me_block, 2], wz_s.at[3], wz_r.at[3], {"zh": by}),
    ]

    def send_pieces(*pieces):
        for p in pieces:
            for slot in (NEAR, FAR, PARTNER):
                go(piece(p, slot), gives[slot])

    go(wz[0])
    send_pieces(IDS, 0, 1)
    go(wz[1])
    go(wz[2])

    for copy in local:
        copy.wait()
    for i in range(rows // 128):
        wide = jnp.broadcast_to(idr[OWN, 0:1, i * 128:(i + 1) * 128].astype(jnp.float32), (128, 128))
        qid[i * 128:(i + 1) * 128, :] = jnp.transpose(wide)

    def attn(slot, head, first=False):
        def body(t, carry):
            at = pl.ds(pl.multiple_of(t * tr, tr), tr)
            q = qv[at, head * HD:(head + 1) * HD]
            scores = lax.dot_general(
                q, kv[slot, 2 * head], (((1,), (1,)), ((), ())), preferred_element_type=jnp.float32
            )
            n = rows // HD
            mine = tile_lanes(qid[at, :], n)
            theirs = jnp.broadcast_to(idr[slot, 0:1, :].astype(jnp.float32), (tr, rows))
            scores = jnp.where(mine == theirs, scores, NEG)
            top = jnp.broadcast_to(jnp.max(scores, axis=1, keepdims=True), (tr, HD))
            if not first:
                old = m_sc[at, :]
                top = jnp.maximum(old, top)
            weights = jnp.exp2((scores - tile_lanes(top, n)) * factor)
            part = weights[:, :HD]
            for i in range(1, n):
                part = part + weights[:, i * HD:(i + 1) * HD]
            summed = jnp.dot(weights.astype(jnp.bfloat16), kv[slot, 2 * head + 1], preferred_element_type=jnp.float32)
            if not first:
                scale = jnp.exp2((old - top) * factor)
                part = part + l_sc[at, :] * scale
                summed = summed + acc_sc[at, :] * scale
            m_sc[at, :] = top
            l_sc[at, :] = part
            acc_sc[at, :] = summed
            return carry

        def run():
            lax.fori_loop(0, CH, body, 0, unroll=True)

        where(gets[slot], run)

    def finish(head, chunk):
        at = pl.ds(chunk * tr, tr)
        total = jnp.sum(l_sc[at, :], axis=1, keepdims=True)
        ag[0, head, at, :] = (acc_sc[at, :] / total).astype(jnp.bfloat16)

    parts = 4
    tp = tr // parts
    ups_of = jnp.where(y_at == 0, 3, jnp.where(y_at == yn - 1, 1, 2))

    def az(head, chunk, kind):
        at = pl.ds(chunk * tr, tr)
        if kind == 0:
            src, dst, to = ag.at[0, head, at], ag.at[1, head, at], z_up
        elif kind == 1:
            src, dst, to = ag.at[0, head, at], ag.at[3, head, at], z_down
        else:
            at = pl.ds(chunk * tr + (kind - 2) * tp, tp)
            upward = kind - 2 < ups_of
            src = ag.at[jnp.where(upward, 1, 3), head, at]
            dst, to = ag.at[2, head, at], jnp.where(upward, z_up, z_down)
        return remote(src, dst, az_s.at[head, chunk, kind], az_r.at[head, chunk, kind], {"zh": to})

    def z_relay(head, chunk):
        for kind in (0, 1):
            az(head, chunk, kind).wait_recv()
        for i in range(parts):
            go(az(head, chunk, 2 + i))

    def z_direct(head, chunk):
        go(az(head, chunk, 0))
        go(az(head, chunk, 1))

    ups, downs = yn // 2, (yn - 1) // 2

    def w_step(kind, t):
        if kind == "up":
            src, sems, to = wblock(-t), (wp_s.at[t], wp_r.at[t]), y_up
        elif kind == "down":
            src, sems, to = wblock(t), (wm_s.at[t], wm_r.at[t]), y_down
        else:
            src, sems, to = wblock(t), (wq_s.at[t % yn], wq_r.at[t % yn]), partner
        block = wg.at[src, pl.ds(1, ZH - 1)]
        return remote(block, block, *sems, {"seq": to})

    def w_advance(t):
        if t >= ups:
            return
        w_step("up", t).wait_recv()
        if t + 1 < ups:
            go(w_step("up", t + 1))
        go(w_step("partner", -1 - t))
        if t < downs:
            w_step("down", t).wait_recv()
            if t + 1 < downs:
                go(w_step("down", t + 1))
            go(w_step("partner", 1 + t))

    def arrive(slot, *pieces):
        for p in pieces:
            where(gets[slot], piece(p, slot).wait_recv)
            if slot == NEAR:
                go(piece(p, RELAY), gives[RELAY])

    attn(OWN, 0, first=True)
    arrive(PARTNER, IDS, 0, 1)
    attn(PARTNER, 0)
    wz[0].wait_recv()
    go(wz[3])
    send_pieces(2, 3)
    arrive(NEAR, IDS, 0, 1)
    attn(NEAR, 0)
    arrive(FAR, IDS, 0, 1)
    attn(FAR, 0)
    arrive(RELAY, IDS, 0, 1)
    attn(RELAY, 0)
    for c in range(CH):
        finish(0, c)
        if c < 3:
            z_direct(0, c)
    for copy in wz[1:]:
        copy.wait_recv()
    go(w_step("up", 0))
    go(w_step("down", 0))
    go(w_step("partner", 0))
    arrive(NEAR, 2, 3)
    attn(OWN, 1, first=True)
    arrive(PARTNER, 2, 3)
    attn(PARTNER, 1)
    attn(NEAR, 1)
    arrive(FAR, 2, 3)
    attn(FAR, 1)
    w_advance(0)
    arrive(RELAY, 2, 3)
    attn(RELAY, 1)
    for c in range(CH):
        finish(1, c)
    z_relay(0, 0)
    z_direct(1, 0)
    z_relay(0, 1)
    z_direct(1, 1)
    w_advance(1)
    z_relay(1, 0)
    z_direct(0, 3)
    z_relay(0, 2)
    w_advance(2)
    z_relay(1, 1)
    z_direct(1, 2)
    w_advance(3)
    z_relay(0, 3)
    z_direct(1, 3)
    w_local.wait()
    for t in range(yn):
        w_step("partner", t).wait_recv()

    def project(c):
        at = pl.ds(c * tr, tr)
        for head in range(2):
            for kind in range(2, 2 + parts):
                az(head, c, kind).wait_recv()
        total = None
        for head in range(2):
            left = jnp.concatenate([ag[r, head, at, :] for r in range(ZH)], axis=1)
            n = wg.shape[0] // 2
            right = jnp.concatenate(
                [wg[head * n:(head + 1) * n, r].reshape(HD, slab) for r in range(ZH)], axis=0
            )
            term = jnp.dot(left, right, preferred_element_type=jnp.float32)
            total = term if total is None else total + term
        xs[c] = jnp.transpose(total).astype(jnp.bfloat16).reshape(xn, own, tr)
        for r in range(1, xn):
            go(x_copy(c, r))

    def x_copy(c, r):
        to = lax.rem(x_at + r, xn)
        return remote(xs.at[c, to], xr.at[c, r - 1], x_s.at[c, r - 1], x_r.at[c, r - 1], {"x": to})

    def out_copy(c):
        return pltpu.make_async_copy(ot.at[c], out_hbm.at[:, pl.ds(c * tr, tr)], o_s.at[c])

    def mix(c):
        total = xs[c, x_at].astype(jnp.float32)
        for r in range(1, xn):
            x_copy(c, r).wait_recv()
            total = total + xr[c, r - 1].astype(jnp.float32)
        ot[c] = total.astype(jnp.bfloat16)
        out_copy(c).start()

    project(0)
    z_relay(1, 2)
    project(1)
    z_relay(1, 3)
    mix(0)
    project(2)
    mix(1)
    project(3)
    mix(2)
    mix(3)
    for copy, condition in sent:
        where(condition, copy.wait_send)
    for c in range(CH):
        out_copy(c).wait()


def shards(yn, xn, queries, keys, values, segment_ids, out_weight):
    rows = queries.shape[0]
    depth, features = out_weight.shape
    own = features // (ZH * xn)
    slab = features // ZH
    wb = depth // (2 * yn)
    ids = segment_ids.reshape(1, rows)
    weight = out_weight.reshape(2 * yn, wb, features)
    dma = pltpu.SemaphoreType.DMA
    bf16, f32 = jnp.bfloat16, jnp.float32
    hbm = pl.BlockSpec(memory_space=pl.ANY)
    ups, downs = yn // 2, max(1, (yn - 1) // 2)
    out = pl.pallas_call(
        functools.partial(kernel, yn, xn),
        out_shape=jax.ShapeDtypeStruct((own, rows), bf16),
        in_specs=[hbm] * 5,
        out_specs=hbm,
        scratch_shapes=[
            pltpu.VMEM((rows, 2 * HD), bf16),
            pltpu.VMEM((5, 4, rows, HD), bf16),
            pltpu.VMEM((5, 1, rows), jnp.int32),
            pltpu.VMEM((rows, HD), f32),
            pltpu.VMEM((rows, HD), f32),
            pltpu.VMEM((rows, HD), f32),
            pltpu.VMEM((rows, HD), f32),
            pltpu.VMEM((ZH, 2, rows, HD), bf16),
            pltpu.VMEM((2 * yn, ZH, wb, slab), bf16),
            pltpu.VMEM((wb, slab), bf16),
            pltpu.VMEM((CH, xn, own, rows // CH), bf16),
            pltpu.VMEM((CH, xn - 1, own, rows // CH), bf16),
            pltpu.VMEM((CH, own, rows // CH), bf16),
            dma((5, 4)), dma((5, 4)),
            dma((4,)), dma((4,)),
            dma((ups,)), dma((ups,)),
            dma((downs,)), dma((downs,)),
            dma((yn,)), dma((yn,)),
            dma((2, CH, 6)), dma((2, CH, 6)),
            dma((CH, xn - 1)), dma((CH, xn - 1)),
            dma((CH,)), dma((7,)),
        ],
        compiler_params=pltpu.CompilerParams(
            collective_id=0, has_side_effects=True, vmem_limit_bytes=60 * 1024 * 1024
        ),
    )(queries, keys, values, ids, weight)
    return jnp.transpose(out)


def build(mesh, yn):
    sn, hn = mesh.shape["seq"], mesh.shape["head"]
    torus = Mesh(mesh.devices.reshape(sn, ZH, hn // ZH), ("seq", "zh", "x"))
    head = ("zh", "x")
    in_specs = (P("seq", head), P("seq", head), P("seq", head), P("seq"), P(head, None))
    return jax.shard_map(
        functools.partial(shards, yn, hn // ZH),
        mesh=torus, in_specs=in_specs, out_specs=P("seq", head), check_vma=False,
    )


def solution(mesh):
    return build(mesh, Y)
```

```python
import functools
import math

import jax
import jax.numpy as jnp
from jax import lax
from jax.experimental import pallas as pl
from jax.experimental.pallas import tpu as pltpu
from jax.sharding import Mesh
from jax.sharding import PartitionSpec as P

Y = 8
ZH = 4
HD = 128
CH = 4
NEG = -1e30
MESH = pl.DeviceIdType.MESH
NEAR, FAR, PARTNER, RELAY, OWN = range(5)


def tile_lanes(x, n):
    return jnp.concatenate([x] * n, axis=1)


def kernel(
    yn, xn, q_hbm, k_hbm, v_hbm, ids_hbm, w_hbm, out_hbm,
    qv, kv, idr, qid, m_sc, l_sc, acc_sc, ag, wg, wrelay, xs, xr, ot,
    kv_s, kv_r, id_s, id_r, wz_s, wz_r, w_s, wp_r, wm_r, wq_r, az_s, az_r, x_s, x_r, o_s, loc,
):
    rows = q_hbm.shape[0]
    tr = rows // CH
    slab = w_hbm.shape[2] // ZH
    own = out_hbm.shape[0]
    factor = HD ** -0.5 * math.log2(math.e)

    s_at = lax.axis_index("seq")
    z_at = lax.axis_index("zh")
    x_at = lax.axis_index("x")
    sn = lax.axis_size("seq")
    core = lax.rem(s_at, 2)
    sgn = 2 * core - 1
    near = lax.rem(s_at + sgn + sn, sn)
    far_to = lax.rem(s_at - 2 * sgn + sn, sn)
    far_from = lax.rem(s_at + 2 * sgn + sn, sn)
    partner = s_at - sgn
    y_at = lax.rem(s_at // 2, yn)
    line = (s_at // (2 * yn)) * (2 * yn)
    y_up = line + lax.rem(y_at + 1, yn) * 2 + core
    y_down = line + lax.rem(y_at + yn - 1, yn) * 2 + core
    z_up = lax.rem(z_at + 1, ZH)
    z_two = lax.rem(z_at + 2, ZH)
    z_down = lax.rem(z_at + ZH - 1, ZH)

    def wblock(distance):
        return lax.rem(y_at + distance + 2 * yn, yn) * 2 + core

    me_block = 2 * y_at + core

    def remote(src, dst, send, recv, device):
        return pltpu.make_async_remote_copy(
            src_ref=src, dst_ref=dst, send_sem=send, recv_sem=recv,
            device_id=device, device_id_type=MESH,
        )

    outer = jnp.logical_and(s_at + sgn >= 0, s_at + sgn < sn)
    inner = jnp.logical_and(s_at - 2 * sgn >= 0, s_at - 2 * sgn < sn)
    gives = {NEAR: outer, FAR: inner, PARTNER: None, RELAY: outer}
    gets = {NEAR: outer, FAR: outer, PARTNER: None, RELAY: inner, OWN: None}
    targets = {NEAR: {"seq": near}, FAR: {"seq": far_to}, PARTNER: {"seq": partner}, RELAY: {"seq": partner}}

    def where(condition, act):
        if condition is None:
            act()
        else:
            pl.when(condition)(act)

    def taken(ref, sem):
        return remote(ref, ref, sem, sem, {"seq": partner}).wait_recv

    def given(ref, sem):
        return remote(ref, ref, sem, sem, {"seq": partner}).wait_send

    def piece_src(p):
        src = k_hbm if p % 2 == 0 else v_hbm
        return src.at[:, pl.ds((p // 2) * HD, HD)]

    def piece(p, slot):
        return remote(piece_src(p), kv.at[slot, p], kv_s.at[slot], kv_r.at[slot, p // 2], targets[slot])

    def relayed(head):
        pair = pl.ds(2 * head, 2)
        return remote(kv.at[NEAR, pair], kv.at[RELAY, pair], kv_s.at[RELAY], kv_r.at[RELAY, head], targets[RELAY])

    def marks(slot):
        src = idr.at[NEAR] if slot == RELAY else ids_hbm
        return remote(src, idr.at[slot], id_s.at[slot], id_r.at[slot], targets[slot])

    def cols(z):
        return pl.ds(pl.multiple_of(z * slab, 128), slab)

    local = [pltpu.make_async_copy(piece_src(p), kv.at[OWN, p], loc.at[0]) for p in range(4)]
    local.append(pltpu.make_async_copy(ids_hbm, idr.at[OWN], loc.at[1]))
    local.append(pltpu.make_async_copy(q_hbm, qv, loc.at[2]))
    w_local = pltpu.make_async_copy(w_hbm.at[:, :, cols(z_at)], wg.at[:, 0], loc.at[3])
    for copy in local:
        copy.start()
    w_local.start()

    barrier = pltpu.get_barrier_semaphore()
    peers = [{"seq": near}, {"seq": partner}, {"seq": far_to}, {"seq": far_from}, {"seq": y_up}, {"seq": y_down},
             {"zh": z_up}, {"zh": z_down}]
    peers += [{"x": lax.rem(x_at + r, xn)} for r in range(1, xn)]
    for peer in peers:
        pl.semaphore_signal(barrier, inc=1, device_id=peer, device_id_type=MESH)
    pl.semaphore_wait(barrier, len(peers))

    upper, lower = y_at == yn - 1, y_at == 0
    by = jnp.where(jnp.logical_or(lower, jnp.logical_and(core == 0, jnp.logical_not(upper))), z_up, z_down)
    wz = [
        remote(w_hbm.at[me_block, :, cols(z_two)], wrelay, wz_s.at[0], wz_r.at[0], {"zh": by}),
        remote(w_hbm.at[me_block, :, cols(z_up)], wg.at[me_block, 1], wz_s.at[0], wz_r.at[1], {"zh": z_up}),
        remote(w_hbm.at[me_block, :, cols(z_down)], wg.at[me_block, 3], wz_s.at[0], wz_r.at[1], {"zh": z_down}),
        remote(wrelay, wg.at[me_block, 2], wz_s.at[0], wz_r.at[1], {"zh": by}),
    ]

    def send_pieces(*pieces):
        for p in pieces:
            for slot in (NEAR, FAR, PARTNER):
                where(gives[slot], piece(p, slot).start)

    wz[0].start()
    for slot in (NEAR, FAR, PARTNER):
        where(gives[slot], marks(slot).start)
    send_pieces(0, 1)
    wz[1].start()
    wz[2].start()

    pltpu.make_async_copy(kv.at[OWN], kv.at[OWN], loc.at[0]).wait()
    for copy in local[4:]:
        copy.wait()
    for i in range(rows // 128):
        wide = jnp.broadcast_to(idr[OWN, 0:1, i * 128:(i + 1) * 128].astype(jnp.float32), (128, 128))
        qid[i * 128:(i + 1) * 128, :] = jnp.transpose(wide)

    def attn(slot, head, chunks=range(CH), first=False):
        def body(t):
            at = pl.ds(t * tr, tr)
            q = qv[at, head * HD:(head + 1) * HD]
            scores = lax.dot_general(
                q, kv[slot, 2 * head], (((1,), (1,)), ((), ())), preferred_element_type=jnp.float32
            )
            n = rows // HD
            mine = tile_lanes(qid[at, :], n)
            theirs = jnp.broadcast_to(idr[slot, 0:1, :].astype(jnp.float32), (tr, rows))
            scores = jnp.where(mine == theirs, scores, NEG)
            top = jnp.broadcast_to(jnp.max(scores, axis=1, keepdims=True), (tr, HD))
            if not first:
                old = m_sc[at, :]
                top = jnp.maximum(old, top)
            weights = jnp.exp2((scores - tile_lanes(top, n)) * factor)
            part = weights[:, :HD]
            for i in range(1, n):
                part = part + weights[:, i * HD:(i + 1) * HD]
            summed = jnp.dot(weights.astype(jnp.bfloat16), kv[slot, 2 * head + 1], preferred_element_type=jnp.float32)
            if not first:
                scale = jnp.exp2((old - top) * factor)
                part = part + l_sc[at, :] * scale
                summed = summed + acc_sc[at, :] * scale
            m_sc[at, :] = top
            l_sc[at, :] = part
            acc_sc[at, :] = summed

        def run():
            for t in chunks:
                body(t)

        where(gets[slot], run)

    def finish(head, chunk):
        at = pl.ds(chunk * tr, tr)
        total = jnp.sum(l_sc[at, :], axis=1, keepdims=True)
        ag[0, head, at, :] = (acc_sc[at, :] / total).astype(jnp.bfloat16)

    parts = 4
    tp = tr // parts
    ups_of = jnp.where(lower, 3, jnp.where(upper, 1, 2))

    def az(head, chunk, kind):
        at = pl.ds(chunk * tr, tr)
        arrived = az_r.at[head, chunk, 0]
        if kind == 0:
            src, dst, to = ag.at[0, head, at], ag.at[1, head, at], z_up
        elif kind == 1:
            src, dst, to = ag.at[0, head, at], ag.at[3, head, at], z_down
        else:
            at = pl.ds(chunk * tr + (kind - 2) * tp, tp)
            upward = kind - 2 < ups_of
            src = ag.at[jnp.where(upward, 1, 3), head, at]
            dst, to = ag.at[2, head, at], jnp.where(upward, z_up, z_down)
            arrived = az_r.at[head, chunk, 1]
        return remote(src, dst, az_s.at[0], arrived, {"zh": to})

    def z_relay(head, chunk):
        at = pl.ds(chunk * tr, tr)
        taken(ag.at[pl.ds(0, 2), head, at], az_r.at[head, chunk, 0])()
        for i in range(parts):
            az(head, chunk, 2 + i).start()

    def z_direct(head, chunk):
        az(head, chunk, 0).start()
        az(head, chunk, 1).start()

    ups, downs = yn // 2, (yn - 1) // 2

    def w_step(kind, t):
        if kind == "up":
            src, arrived, to = wblock(-t), wp_r.at[t], y_up
        elif kind == "down":
            src, arrived, to = wblock(t), wm_r.at[t], y_down
        else:
            src, arrived, to = wblock(t), wq_r.at[0], partner
        block = wg.at[src, pl.ds(1, ZH - 1)]
        return remote(block, block, w_s.at[0], arrived, {"seq": to})

    def w_advance(t):
        if t >= ups:
            return
        w_step("up", t).wait_recv()
        if t + 1 < ups:
            w_step("up", t + 1).start()
        w_step("partner", -1 - t).start()
        if t < downs:
            w_step("down", t).wait_recv()
            if t + 1 < downs:
                w_step("down", t + 1).start()
            w_step("partner", 1 + t).start()

    def arrive(slot, head):
        def act():
            if head == 0:
                marks(slot).wait_recv()
                if slot == NEAR:
                    marks(RELAY).start()
            taken(kv.at[slot, pl.ds(2 * head, 2)], kv_r.at[slot, head])()
            if slot == NEAR:
                relayed(head).start()

        where(gets[slot], act)

    attn(OWN, 0, first=True)
    arrive(PARTNER, 0)
    attn(PARTNER, 0)
    wz[0].wait_recv()
    wz[3].start()
    send_pieces(2)
    arrive(NEAR, 0)
    attn(NEAR, 0)
    taken(wg.at[me_block, pl.ds(1, ZH - 1)], wz_r.at[1])()
    w_step("up", 0).start()
    w_step("down", 0).start()
    w_step("partner", 0).start()
    send_pieces(3)
    arrive(FAR, 0)
    arrive(RELAY, 0)
    for c in range(CH):
        attn(FAR, 0, (c,))
        attn(RELAY, 0, (c,))
        finish(0, c)
        z_direct(0, c)
    w_advance(0)
    attn(OWN, 1, first=True)
    arrive(PARTNER, 1)
    attn(PARTNER, 1)
    arrive(NEAR, 1)
    attn(NEAR, 1)
    z_relay(0, 0)
    arrive(FAR, 1)
    attn(FAR, 1)
    w_advance(1)
    z_relay(0, 1)
    arrive(RELAY, 1)
    for c in range(CH):
        attn(RELAY, 1, (c,))
        finish(1, c)
        if c < 2:
            z_direct(1, c)
    w_advance(2)
    z_relay(0, 2)
    z_relay(1, 0)
    z_direct(1, 2)
    w_advance(3)
    z_relay(0, 3)
    z_relay(1, 1)
    z_direct(1, 3)
    w_local.wait()
    taken(wg.at[pl.ds(0, yn), pl.ds(1, ZH - 1)], wq_r.at[0])()

    def project(c):
        at = pl.ds(c * tr, tr)
        for head in range(2):
            taken(ag.at[2, head, at], az_r.at[head, c, 1])()
        total = None
        for head in range(2):
            left = jnp.concatenate([ag[r, head, at, :] for r in range(ZH)], axis=1)
            n = wg.shape[0] // 2
            right = jnp.concatenate(
                [wg[head * n:(head + 1) * n, r].reshape(HD, slab) for r in range(ZH)], axis=0
            )
            term = jnp.dot(left, right, preferred_element_type=jnp.float32)
            total = term if total is None else total + term
        xs[c] = jnp.transpose(total).astype(jnp.bfloat16).reshape(xn, own, tr)
        for r in range(1, xn):
            x_copy(c, r).start()

    def x_copy(c, r):
        to = lax.rem(x_at + r, xn)
        return remote(xs.at[c, to], xr.at[c, r - 1], x_s.at[0], x_r.at[c], {"x": to})

    def out_copy(c):
        return pltpu.make_async_copy(ot.at[c], out_hbm.at[:, pl.ds(c * tr, tr)], o_s.at[0])

    def mix(c):
        total = xs[c, x_at].astype(jnp.float32)
        taken(xr.at[c], x_r.at[c])()
        for r in range(1, xn):
            total = total + xr[c, r - 1].astype(jnp.float32)
        ot[c] = total.astype(jnp.bfloat16)
        out_copy(c).start()

    project(0)
    z_relay(1, 2)
    project(1)
    z_relay(1, 3)
    mix(0)
    project(2)
    mix(1)
    project(3)
    mix(2)
    mix(3)
    for slot in (NEAR, FAR, PARTNER, RELAY):
        where(gives[slot], marks(slot).wait_send)
        where(gives[slot], given(kv.at[slot], kv_s.at[slot]))
    given(wg.at[0], wz_s.at[0])()
    given(wg.at[pl.ds(0, 2 * yn - 1), pl.ds(1, ZH - 1)], w_s.at[0])()
    given(ag.at[pl.ds(0, 3)], az_s.at[0])()
    given(xr, x_s.at[0])()
    pltpu.make_async_copy(ot, ot, o_s.at[0]).wait()


def shards(yn, xn, queries, keys, values, segment_ids, out_weight):
    rows = queries.shape[0]
    depth, features = out_weight.shape
    own = features // (ZH * xn)
    slab = features // ZH
    wb = depth // (2 * yn)
    ids = segment_ids.reshape(1, rows)
    weight = out_weight.reshape(2 * yn, wb, features)
    dma = pltpu.SemaphoreType.DMA
    bf16, f32 = jnp.bfloat16, jnp.float32
    hbm = pl.BlockSpec(memory_space=pl.ANY)
    ups, downs = yn // 2, max(1, (yn - 1) // 2)
    out = pl.pallas_call(
        functools.partial(kernel, yn, xn),
        out_shape=jax.ShapeDtypeStruct((own, rows), bf16),
        in_specs=[hbm] * 5,
        out_specs=hbm,
        scratch_shapes=[
            pltpu.VMEM((rows, 2 * HD), bf16),
            pltpu.VMEM((5, 4, rows, HD), bf16),
            pltpu.VMEM((5, 1, rows), jnp.int32),
            pltpu.VMEM((rows, HD), f32),
            pltpu.VMEM((rows, HD), f32),
            pltpu.VMEM((rows, HD), f32),
            pltpu.VMEM((rows, HD), f32),
            pltpu.VMEM((ZH, 2, rows, HD), bf16),
            pltpu.VMEM((2 * yn, ZH, wb, slab), bf16),
            pltpu.VMEM((wb, slab), bf16),
            pltpu.VMEM((CH, xn, own, rows // CH), bf16),
            pltpu.VMEM((CH, xn - 1, own, rows // CH), bf16),
            pltpu.VMEM((CH, own, rows // CH), bf16),
            dma((4,)), dma((4, 2)), dma((4,)), dma((4,)),
            dma((1,)), dma((2,)),
            dma((1,)), dma((ups,)), dma((downs,)), dma((1,)),
            dma((1,)), dma((2, CH, 2)),
            dma((1,)), dma((CH,)),
            dma((1,)), dma((4,)),
        ],
        compiler_params=pltpu.CompilerParams(
            collective_id=0, has_side_effects=True, vmem_limit_bytes=60 * 1024 * 1024
        ),
    )(queries, keys, values, ids, weight)
    return jnp.transpose(out)


def build(mesh, yn):
    sn, hn = mesh.shape["seq"], mesh.shape["head"]
    torus = Mesh(mesh.devices.reshape(sn, ZH, hn // ZH), ("seq", "zh", "x"))
    head = ("zh", "x")
    in_specs = (P("seq", head), P("seq", head), P("seq", head), P("seq"), P(head, None))
    return jax.shard_map(
        functools.partial(shards, yn, hn // ZH),
        mesh=torus, in_specs=in_specs, out_specs=P("seq", head), check_vma=False,
    )


def solution(mesh):
    return build(mesh, Y)
```

```python
import functools
import math

import jax
import jax.numpy as jnp
from jax import lax
from jax.experimental import pallas as pl
from jax.experimental.pallas import tpu as pltpu
from jax.sharding import Mesh
from jax.sharding import PartitionSpec as P

Y = 8
ZH = 4
HD = 128
CH = 4
NEG = -1e30
MESH = pl.DeviceIdType.MESH
NEAR, FAR, PARTNER, RELAY, OWN = range(5)


def tile_lanes(x, n):
    return jnp.concatenate([x] * n, axis=1)


def kernel(
    yn, xn, q_hbm, k_hbm, v_hbm, ids_hbm, w_hbm, out_hbm,
    qv, kv, idr, qid, m_sc, l_sc, acc_sc, ag, wg, wrelay, xs,
    kv_s, kv_r, id_s, id_r, wz_s, wz_r, w_s, wp_r, wm_r, wq_r, az_s, az_r, x_s, x_r, o_s, loc,
):
    rows = q_hbm.shape[0]
    tr = rows // CH
    slab = w_hbm.shape[2] // ZH
    own = out_hbm.shape[1]
    factor = HD ** -0.5 * math.log2(math.e)

    s_at = lax.axis_index("seq")
    z_at = lax.axis_index("zh")
    x_at = lax.axis_index("x")
    sn = lax.axis_size("seq")
    core = lax.rem(s_at, 2)
    sgn = 2 * core - 1
    near = lax.rem(s_at + sgn + sn, sn)
    far_to = lax.rem(s_at - 2 * sgn + sn, sn)
    far_from = lax.rem(s_at + 2 * sgn + sn, sn)
    partner = s_at - sgn
    y_at = lax.rem(s_at // 2, yn)
    line = (s_at // (2 * yn)) * (2 * yn)
    y_up = line + lax.rem(y_at + 1, yn) * 2 + core
    y_down = line + lax.rem(y_at + yn - 1, yn) * 2 + core
    z_up = lax.rem(z_at + 1, ZH)
    z_two = lax.rem(z_at + 2, ZH)
    z_down = lax.rem(z_at + ZH - 1, ZH)

    def wblock(distance):
        return lax.rem(y_at + distance + 2 * yn, yn) * 2 + core

    me_block = 2 * y_at + core

    def remote(src, dst, send, recv, device):
        return pltpu.make_async_remote_copy(
            src_ref=src, dst_ref=dst, send_sem=send, recv_sem=recv,
            device_id=device, device_id_type=MESH,
        )

    outer = jnp.logical_and(s_at + sgn >= 0, s_at + sgn < sn)
    inner = jnp.logical_and(s_at - 2 * sgn >= 0, s_at - 2 * sgn < sn)
    gives = {NEAR: outer, FAR: inner, PARTNER: None, RELAY: outer}
    gets = {NEAR: outer, FAR: outer, PARTNER: None, RELAY: inner, OWN: None}
    targets = {NEAR: {"seq": near}, FAR: {"seq": far_to}, PARTNER: {"seq": partner}, RELAY: {"seq": partner}}

    def where(condition, act):
        if condition is None:
            act()
        else:
            pl.when(condition)(act)

    def taken(ref, sem):
        return remote(ref, ref, sem, sem, {"seq": partner}).wait_recv

    def given(ref, sem):
        return remote(ref, ref, sem, sem, {"seq": partner}).wait_send

    def piece_src(p):
        src = k_hbm if p % 2 == 0 else v_hbm
        return src.at[:, pl.ds((p // 2) * HD, HD)]

    def piece(p, slot):
        return remote(piece_src(p), kv.at[slot, p], kv_s.at[slot], kv_r.at[slot, p // 2], targets[slot])

    def relayed(head):
        pair = pl.ds(2 * head, 2)
        return remote(kv.at[NEAR, pair], kv.at[RELAY, pair], kv_s.at[RELAY], kv_r.at[RELAY, head], targets[RELAY])

    def marks(slot):
        src = idr.at[NEAR] if slot == RELAY else ids_hbm
        return remote(src, idr.at[slot], id_s.at[slot], id_r.at[slot], targets[slot])

    def cols(z):
        return pl.ds(pl.multiple_of(z * slab, 128), slab)

    local = [pltpu.make_async_copy(piece_src(p), kv.at[OWN, p], loc.at[0]) for p in range(4)]
    local.append(pltpu.make_async_copy(ids_hbm, idr.at[OWN], loc.at[1]))
    local.append(pltpu.make_async_copy(q_hbm, qv, loc.at[2]))
    w_local = pltpu.make_async_copy(w_hbm.at[:, :, cols(z_at)], wg.at[:, 0], loc.at[3])
    barrier = pltpu.get_barrier_semaphore()
    peers = [{"seq": near}, {"seq": partner}, {"seq": far_to}, {"seq": far_from}, {"seq": y_up}, {"seq": y_down},
             {"zh": z_up}, {"zh": z_down}]
    peers += [{"x": lax.rem(x_at + r, xn)} for r in range(1, xn)]
    for peer in peers:
        pl.semaphore_signal(barrier, inc=1, device_id=peer, device_id_type=MESH)
    for copy in local:
        copy.start()
    w_local.start()
    pl.semaphore_wait(barrier, len(peers))

    upper, lower = y_at == yn - 1, y_at == 0
    by = jnp.where(jnp.logical_or(lower, jnp.logical_and(core == 0, jnp.logical_not(upper))), z_up, z_down)
    wz = [
        remote(w_hbm.at[me_block, :, cols(z_two)], wrelay, wz_s.at[0], wz_r.at[0], {"zh": by}),
        remote(w_hbm.at[me_block, :, cols(z_up)], wg.at[me_block, 1], wz_s.at[0], wz_r.at[1], {"zh": z_up}),
        remote(w_hbm.at[me_block, :, cols(z_down)], wg.at[me_block, 3], wz_s.at[0], wz_r.at[1], {"zh": z_down}),
        remote(wrelay, wg.at[me_block, 2], wz_s.at[0], wz_r.at[1], {"zh": by}),
    ]

    def send_pieces(*pieces):
        for p in pieces:
            for slot in (NEAR, FAR, PARTNER):
                where(gives[slot], piece(p, slot).start)

    wz[0].start()
    for slot in (NEAR, FAR, PARTNER):
        where(gives[slot], marks(slot).start)
    send_pieces(0, 1)
    wz[1].start()
    wz[2].start()

    pltpu.make_async_copy(kv.at[OWN], kv.at[OWN], loc.at[0]).wait()
    for copy in local[4:]:
        copy.wait()
    for i in range(rows // 128):
        wide = jnp.broadcast_to(idr[OWN, 0:1, i * 128:(i + 1) * 128].astype(jnp.float32), (128, 128))
        qid[i * 128:(i + 1) * 128, :] = jnp.transpose(wide)

    def attn(slot, head, chunks=range(CH), first=False):
        def body(t):
            at = pl.ds(t * tr, tr)
            q = qv[at, head * HD:(head + 1) * HD]
            scores = lax.dot_general(
                q, kv[slot, 2 * head], (((1,), (1,)), ((), ())), preferred_element_type=jnp.float32
            )
            n = rows // HD
            mine = tile_lanes(qid[at, :], n)
            theirs = jnp.broadcast_to(idr[slot, 0:1, :].astype(jnp.float32), (tr, rows))
            scores = jnp.where(mine == theirs, scores, NEG)
            top = jnp.broadcast_to(jnp.max(scores, axis=1, keepdims=True), (tr, HD))
            if not first:
                old = m_sc[at, :]
                top = jnp.maximum(old, top)
            weights = jnp.exp2((scores - tile_lanes(top, n)) * factor)
            part = weights[:, :HD]
            for i in range(1, n):
                part = part + weights[:, i * HD:(i + 1) * HD]
            summed = jnp.dot(weights.astype(jnp.bfloat16), kv[slot, 2 * head + 1], preferred_element_type=jnp.float32)
            if not first:
                scale = jnp.exp2((old - top) * factor)
                part = part + l_sc[at, :] * scale
                summed = summed + acc_sc[at, :] * scale
            m_sc[at, :] = top
            l_sc[at, :] = part
            acc_sc[at, :] = summed

        def run():
            for t in chunks:
                body(t)

        where(gets[slot], run)

    def finish(head, chunk):
        at = pl.ds(chunk * tr, tr)
        total = jnp.sum(l_sc[at, :], axis=1, keepdims=True)
        ag[0, head, at, :] = (acc_sc[at, :] / total).astype(jnp.bfloat16)

    def turn(chunk):
        return jnp.where(upper, 1 - chunk % 2, chunk % 2)

    def az(head, chunk, kind):
        at = pl.ds(chunk * tr, tr)
        way = turn(chunk) if kind == 2 else kind
        rel, to = 1 + 2 * way, jnp.where(way == 0, z_up, z_down)
        src, dst = (rel, 2) if kind == 2 else (0, rel)
        return remote(
            ag.at[src, head, at], ag.at[dst, head, at], az_s.at[0], az_r.at[head, chunk, kind], {"zh": to}
        )

    def came(head, chunk, way):
        taken(ag.at[0, head, pl.ds(chunk * tr, tr)], az_r.at[head, chunk, way])()

    def z_relay(head, chunk):
        came(head, chunk, turn(chunk))
        az(head, chunk, 2).start()

    def z_direct(head, chunk):
        az(head, chunk, 0).start()
        az(head, chunk, 1).start()

    ups, downs = yn // 2, (yn - 1) // 2

    def w_step(kind, t):
        if kind == "up":
            src, arrived, to = wblock(-t), wp_r.at[t], y_up
        elif kind == "down":
            src, arrived, to = wblock(t), wm_r.at[t], y_down
        else:
            src, arrived, to = wblock(t), wq_r.at[0], partner
        block = wg.at[src, pl.ds(1, ZH - 1)]
        return remote(block, block, w_s.at[0], arrived, {"seq": to})

    def w_advance(t):
        if t >= ups:
            return
        w_step("up", t).wait_recv()
        if t + 1 < ups:
            w_step("up", t + 1).start()
        w_step("partner", -1 - t).start()
        if t < downs:
            w_step("down", t).wait_recv()
            if t + 1 < downs:
                w_step("down", t + 1).start()
            w_step("partner", 1 + t).start()

    def arrive(slot, head):
        def act():
            if head == 0:
                marks(slot).wait_recv()
                if slot == NEAR:
                    marks(RELAY).start()
            taken(kv.at[slot, pl.ds(2 * head, 2)], kv_r.at[slot, head])()
            if slot == NEAR:
                relayed(head).start()

        where(gets[slot], act)

    attn(OWN, 0, first=True)
    arrive(PARTNER, 0)
    attn(PARTNER, 0)
    wz[0].wait_recv()
    wz[3].start()
    send_pieces(2)
    arrive(NEAR, 0)
    attn(NEAR, 0)
    taken(wg.at[me_block, pl.ds(1, ZH - 1)], wz_r.at[1])()
    w_step("up", 0).start()
    w_step("down", 0).start()
    w_step("partner", 0).start()
    send_pieces(3)
    arrive(FAR, 0)
    arrive(RELAY, 0)
    for c in range(CH):
        attn(FAR, 0, (c,))
        attn(RELAY, 0, (c,))
        finish(0, c)
        if c < 3:
            z_direct(0, c)
    attn(OWN, 1, first=True)
    arrive(PARTNER, 1)
    attn(PARTNER, 1)
    w_advance(0)
    z_relay(0, 0)
    arrive(NEAR, 1)
    arrive(FAR, 1)
    arrive(RELAY, 1)
    for c in range(CH):
        attn(NEAR, 1, (c,))
        attn(FAR, 1, (c,))
        attn(RELAY, 1, (c,))
        finish(1, c)
        if c < 2:
            z_direct(1, c)
        if c == 1:
            z_relay(0, 1)
            w_advance(1)
    w_advance(2)
    z_relay(1, 0)
    z_direct(0, 3)
    z_relay(0, 2)
    z_direct(1, 2)
    w_advance(3)
    z_relay(1, 1)
    z_relay(0, 3)
    z_direct(1, 3)
    w_local.wait()
    taken(wg.at[pl.ds(0, yn), pl.ds(1, ZH - 1)], wq_r.at[0])()

    def project(c):
        at = pl.ds(c * tr, tr)
        for head in range(2):
            came(head, c, 1 - turn(c))
            az(head, c, 2).wait_recv()
        total = None
        for head in range(2):
            left = jnp.concatenate([ag[r, head, at, :] for r in range(ZH)], axis=1)
            n = wg.shape[0] // 2
            right = jnp.concatenate(
                [wg[head * n:(head + 1) * n, r].reshape(HD, slab) for r in range(ZH)], axis=0
            )
            term = jnp.dot(left, right, preferred_element_type=jnp.float32)
            total = term if total is None else total + term
        xs[c] = jnp.transpose(total).astype(jnp.bfloat16).reshape(xn, own, tr)
        for r in range(1, xn):
            x_copy(c, r).start()
        own_copy(c).start()

    def block(c):
        return pl.ds(c * tr, tr)

    def x_copy(c, r):
        to = lax.rem(x_at + r, xn)
        return remote(xs.at[c, to], out_hbm.at[r, :, block(c)], x_s.at[0], x_r.at[0], {"x": to})

    def own_copy(c):
        return pltpu.make_async_copy(xs.at[c, x_at], out_hbm.at[0, :, block(c)], o_s.at[0])

    project(0)
    z_relay(1, 2)
    project(1)
    z_relay(1, 3)
    project(2)
    project(3)
    taken(out_hbm.at[pl.ds(1, xn - 1)], x_r.at[0])()
    for slot in (NEAR, FAR, PARTNER, RELAY):
        where(gives[slot], marks(slot).wait_send)
        where(gives[slot], given(kv.at[slot], kv_s.at[slot]))
    given(wg.at[0], wz_s.at[0])()
    given(wg.at[pl.ds(0, 2 * yn - 1), pl.ds(1, ZH - 1)], w_s.at[0])()
    given(ag.at[pl.ds(0, 3)], az_s.at[0])()
    given(out_hbm.at[pl.ds(1, xn - 1)], x_s.at[0])()
    pltpu.make_async_copy(out_hbm.at[0], out_hbm.at[0], o_s.at[0]).wait()


def shards(yn, xn, queries, keys, values, segment_ids, out_weight):
    rows = queries.shape[0]
    depth, features = out_weight.shape
    own = features // (ZH * xn)
    slab = features // ZH
    wb = depth // (2 * yn)
    ids = segment_ids.reshape(1, rows)
    weight = out_weight.reshape(2 * yn, wb, features)
    dma = pltpu.SemaphoreType.DMA
    bf16, f32 = jnp.bfloat16, jnp.float32
    hbm = pl.BlockSpec(memory_space=pl.ANY)
    ups, downs = yn // 2, max(1, (yn - 1) // 2)
    out = pl.pallas_call(
        functools.partial(kernel, yn, xn),
        out_shape=jax.ShapeDtypeStruct((xn, own, rows), bf16),
        in_specs=[hbm] * 5,
        out_specs=hbm,
        scratch_shapes=[
            pltpu.VMEM((rows, 2 * HD), bf16),
            pltpu.VMEM((5, 4, rows, HD), bf16),
            pltpu.VMEM((5, 1, rows), jnp.int32),
            pltpu.VMEM((rows, HD), f32),
            pltpu.VMEM((rows, HD), f32),
            pltpu.VMEM((rows, HD), f32),
            pltpu.VMEM((rows, HD), f32),
            pltpu.VMEM((ZH, 2, rows, HD), bf16),
            pltpu.VMEM((2 * yn, ZH, wb, slab), bf16),
            pltpu.VMEM((wb, slab), bf16),
            pltpu.VMEM((CH, xn, own, rows // CH), bf16),
            dma((4,)), dma((4, 2)), dma((4,)), dma((4,)),
            dma((1,)), dma((2,)),
            dma((1,)), dma((ups,)), dma((downs,)), dma((1,)),
            dma((1,)), dma((2, CH, 3)),
            dma((1,)), dma((1,)),
            dma((1,)), dma((4,)),
        ],
        compiler_params=pltpu.CompilerParams(
            collective_id=0, has_side_effects=True, vmem_limit_bytes=60 * 1024 * 1024
        ),
    )(queries, keys, values, ids, weight)
    total = out[0].astype(f32)
    for r in range(1, xn):
        total = total + out[r].astype(f32)
    return jnp.transpose(total.astype(bf16))


def build(mesh, yn):
    sn, hn = mesh.shape["seq"], mesh.shape["head"]
    torus = Mesh(mesh.devices.reshape(sn, ZH, hn // ZH), ("seq", "zh", "x"))
    head = ("zh", "x")
    in_specs = (P("seq", head), P("seq", head), P("seq", head), P("seq"), P(head, None))
    return jax.shard_map(
        functools.partial(shards, yn, hn // ZH),
        mesh=torus, in_specs=in_specs, out_specs=P("seq", head), check_vma=False,
    )


def solution(mesh):
    return build(mesh, Y)
```

```python
import functools
import math

import jax
import jax.numpy as jnp
from jax import lax
from jax.experimental import pallas as pl
from jax.experimental.pallas import tpu as pltpu
from jax.sharding import Mesh
from jax.sharding import PartitionSpec as P

Y = 8
ZH = 4
HD = 128
CH = 4
NEG = -1e30
MESH = pl.DeviceIdType.MESH
NEAR, FAR, PARTNER, RELAY, OWN = range(5)


def tile_lanes(x, n):
    return jnp.concatenate([x] * n, axis=1)


def kernel(
    yn, xn, q_hbm, k_hbm, v_hbm, ids_hbm, w_hbm, out_hbm,
    qv, kv, idr, qid, m_sc, l_sc, acc_sc, ag, wg, wrelay, xs, xr, ot,
    kv_s, kv_r, id_s, id_r, wz_s, wz_r, w_s, wp_r, wm_r, wq_r, az_s, az_r, x_s, x_r, o_s, loc,
):
    rows = q_hbm.shape[0]
    tr = rows // CH
    slab = w_hbm.shape[2] // ZH
    own = out_hbm.shape[0]
    factor = HD ** -0.5 * math.log2(math.e)

    s_at = lax.axis_index("seq")
    z_at = lax.axis_index("zh")
    x_at = lax.axis_index("x")
    sn = lax.axis_size("seq")
    core = lax.rem(s_at, 2)
    sgn = 2 * core - 1
    near = lax.rem(s_at + sgn + sn, sn)
    far_to = lax.rem(s_at - 2 * sgn + sn, sn)
    far_from = lax.rem(s_at + 2 * sgn + sn, sn)
    partner = s_at - sgn
    y_at = lax.rem(s_at // 2, yn)
    line = (s_at // (2 * yn)) * (2 * yn)
    y_up = line + lax.rem(y_at + 1, yn) * 2 + core
    y_down = line + lax.rem(y_at + yn - 1, yn) * 2 + core
    z_up = lax.rem(z_at + 1, ZH)
    z_two = lax.rem(z_at + 2, ZH)
    z_down = lax.rem(z_at + ZH - 1, ZH)

    def wblock(distance):
        return lax.rem(y_at + distance + 2 * yn, yn) * 2 + core

    me_block = 2 * y_at + core

    def remote(src, dst, send, recv, device):
        return pltpu.make_async_remote_copy(
            src_ref=src, dst_ref=dst, send_sem=send, recv_sem=recv,
            device_id=device, device_id_type=MESH,
        )

    outer = jnp.logical_and(s_at + sgn >= 0, s_at + sgn < sn)
    inner = jnp.logical_and(s_at - 2 * sgn >= 0, s_at - 2 * sgn < sn)
    gives = {NEAR: outer, FAR: inner, PARTNER: None, RELAY: outer}
    gets = {NEAR: outer, FAR: outer, PARTNER: None, RELAY: inner, OWN: None}
    targets = {NEAR: {"seq": near}, FAR: {"seq": far_to}, PARTNER: {"seq": partner}, RELAY: {"seq": partner}}

    def where(condition, act):
        if condition is None:
            act()
        else:
            pl.when(condition)(act)

    def taken(ref, sem):
        return remote(ref, ref, sem, sem, {"seq": partner}).wait_recv

    def given(ref, sem):
        return remote(ref, ref, sem, sem, {"seq": partner}).wait_send

    def piece_src(p):
        src = k_hbm if p % 2 == 0 else v_hbm
        return src.at[:, pl.ds((p // 2) * HD, HD)]

    def piece(p, slot):
        return remote(piece_src(p), kv.at[slot, p], kv_s.at[slot], kv_r.at[slot, p // 2], targets[slot])

    def relayed(head):
        pair = pl.ds(2 * head, 2)
        return remote(kv.at[NEAR, pair], kv.at[RELAY, pair], kv_s.at[RELAY], kv_r.at[RELAY, head], targets[RELAY])

    def marks(slot):
        src = idr.at[NEAR] if slot == RELAY else ids_hbm
        return remote(src, idr.at[slot], id_s.at[slot], id_r.at[slot], targets[slot])

    def cols(z):
        return pl.ds(pl.multiple_of(z * slab, 128), slab)

    local = [pltpu.make_async_copy(piece_src(p), kv.at[OWN, p], loc.at[0]) for p in range(4)]
    local.append(pltpu.make_async_copy(ids_hbm, idr.at[OWN], loc.at[1]))
    local.append(pltpu.make_async_copy(q_hbm, qv, loc.at[2]))
    w_local = pltpu.make_async_copy(w_hbm.at[:, :, cols(z_at)], wg.at[:, 0], loc.at[3])
    barrier = pltpu.get_barrier_semaphore()
    peers = [{"seq": near}, {"seq": partner}, {"seq": far_to}, {"seq": far_from}, {"seq": y_up}, {"seq": y_down},
             {"zh": z_up}, {"zh": z_down}]
    peers += [{"x": lax.rem(x_at + r, xn)} for r in range(1, xn)]
    for peer in peers:
        pl.semaphore_signal(barrier, inc=1, device_id=peer, device_id_type=MESH)
    for copy in local:
        copy.start()
    w_local.start()
    pl.semaphore_wait(barrier, len(peers))

    upper, lower = y_at == yn - 1, y_at == 0
    by = jnp.where(jnp.logical_or(lower, jnp.logical_and(core == 0, jnp.logical_not(upper))), z_up, z_down)
    wz = [
        remote(w_hbm.at[me_block, :, cols(z_two)], wrelay, wz_s.at[0], wz_r.at[0], {"zh": by}),
        remote(w_hbm.at[me_block, :, cols(z_up)], wg.at[me_block, 1], wz_s.at[0], wz_r.at[1], {"zh": z_up}),
        remote(w_hbm.at[me_block, :, cols(z_down)], wg.at[me_block, 3], wz_s.at[0], wz_r.at[1], {"zh": z_down}),
        remote(wrelay, wg.at[me_block, 2], wz_s.at[0], wz_r.at[1], {"zh": by}),
    ]

    def send_pieces(*pieces):
        for p in pieces:
            for slot in (NEAR, FAR, PARTNER):
                where(gives[slot], piece(p, slot).start)

    wz[0].start()
    for slot in (NEAR, FAR, PARTNER):
        where(gives[slot], marks(slot).start)
    send_pieces(0, 1)
    wz[1].start()
    wz[2].start()

    pltpu.make_async_copy(kv.at[OWN], kv.at[OWN], loc.at[0]).wait()
    for copy in local[4:]:
        copy.wait()
    for i in range(rows // 128):
        wide = jnp.broadcast_to(idr[OWN, 0:1, i * 128:(i + 1) * 128].astype(jnp.float32), (128, 128))
        qid[i * 128:(i + 1) * 128, :] = jnp.transpose(wide)

    def attn(slot, head, chunks=range(CH), first=False):
        def body(t):
            at = pl.ds(t * tr, tr)
            q = qv[at, head * HD:(head + 1) * HD]
            scores = lax.dot_general(
                q, kv[slot, 2 * head], (((1,), (1,)), ((), ())), preferred_element_type=jnp.float32
            )
            n = rows // HD
            mine = tile_lanes(qid[at, :], n)
            theirs = jnp.broadcast_to(idr[slot, 0:1, :].astype(jnp.float32), (tr, rows))
            scores = jnp.where(mine == theirs, scores, NEG)
            top = jnp.broadcast_to(jnp.max(scores, axis=1, keepdims=True), (tr, HD))
            if not first:
                old = m_sc[at, :]
                top = jnp.maximum(old, top)
            weights = jnp.exp2((scores - tile_lanes(top, n)) * factor)
            part = weights[:, :HD]
            for i in range(1, n):
                part = part + weights[:, i * HD:(i + 1) * HD]
            summed = jnp.dot(weights.astype(jnp.bfloat16), kv[slot, 2 * head + 1], preferred_element_type=jnp.float32)
            if not first:
                scale = jnp.exp2((old - top) * factor)
                part = part + l_sc[at, :] * scale
                summed = summed + acc_sc[at, :] * scale
            m_sc[at, :] = top
            l_sc[at, :] = part
            acc_sc[at, :] = summed

        def run():
            for t in chunks:
                body(t)

        where(gets[slot], run)

    def finish(head, chunk):
        at = pl.ds(chunk * tr, tr)
        total = jnp.sum(l_sc[at, :], axis=1, keepdims=True)
        ag[0, head, at, :] = (acc_sc[at, :] / total).astype(jnp.bfloat16)

    def turn(chunk):
        return jnp.where(upper, 1 - chunk % 2, chunk % 2)

    def az(head, chunk, kind):
        at = pl.ds(chunk * tr, tr)
        way = turn(chunk) if kind == 2 else kind
        rel, to = 1 + 2 * way, jnp.where(way == 0, z_up, z_down)
        src, dst = (rel, 2) if kind == 2 else (0, rel)
        return remote(
            ag.at[src, head, at], ag.at[dst, head, at], az_s.at[0], az_r.at[head, chunk, kind], {"zh": to}
        )

    def came(head, chunk, way):
        taken(ag.at[0, head, pl.ds(chunk * tr, tr)], az_r.at[head, chunk, way])()

    def z_relay(head, chunk):
        came(head, chunk, turn(chunk))
        az(head, chunk, 2).start()

    def z_direct(head, chunk):
        az(head, chunk, 0).start()
        az(head, chunk, 1).start()

    ups, downs = yn // 2, (yn - 1) // 2

    def w_step(kind, t):
        if kind == "up":
            src, arrived, to = wblock(-t), wp_r.at[t], y_up
        elif kind == "down":
            src, arrived, to = wblock(t), wm_r.at[t], y_down
        else:
            src, arrived, to = wblock(t), wq_r.at[0], partner
        block = wg.at[src, pl.ds(1, ZH - 1)]
        return remote(block, block, w_s.at[0], arrived, {"seq": to})

    def w_advance(t):
        if t >= ups:
            return
        w_step("up", t).wait_recv()
        if t + 1 < ups:
            w_step("up", t + 1).start()
        w_step("partner", -1 - t).start()
        if t < downs:
            w_step("down", t).wait_recv()
            if t + 1 < downs:
                w_step("down", t + 1).start()
            w_step("partner", 1 + t).start()

    def arrive(slot, head):
        def act():
            if head == 0:
                marks(slot).wait_recv()
                if slot == NEAR:
                    marks(RELAY).start()
            taken(kv.at[slot, pl.ds(2 * head, 2)], kv_r.at[slot, head])()
            if slot == NEAR:
                relayed(head).start()

        where(gets[slot], act)

    attn(OWN, 0, first=True)
    arrive(PARTNER, 0)
    attn(PARTNER, 0)
    wz[0].wait_recv()
    wz[3].start()
    send_pieces(2)
    arrive(NEAR, 0)
    attn(NEAR, 0)
    arrive(FAR, 0)
    arrive(RELAY, 0)
    for c in range(CH):
        attn(FAR, 0, (c,))
        attn(RELAY, 0, (c,))
        finish(0, c)
        if c < 3:
            z_direct(0, c)
        if c == 0:
            taken(wg.at[me_block, pl.ds(1, ZH - 1)], wz_r.at[1])()
            w_step("up", 0).start()
            w_step("down", 0).start()
            w_step("partner", 0).start()
            send_pieces(3)
    attn(OWN, 1, first=True)
    arrive(PARTNER, 1)
    attn(PARTNER, 1)
    w_advance(0)
    z_relay(0, 0)
    arrive(NEAR, 1)
    arrive(FAR, 1)
    arrive(RELAY, 1)
    for c in range(CH):
        attn(NEAR, 1, (c,))
        attn(FAR, 1, (c,))
        attn(RELAY, 1, (c,))
        finish(1, c)
        if c < 2:
            z_direct(1, c)
        if c == 1:
            z_relay(0, 1)
            w_advance(1)
    w_advance(2)
    z_relay(1, 0)
    z_direct(0, 3)
    z_relay(0, 2)
    z_direct(1, 2)
    w_advance(3)
    z_relay(1, 1)
    z_relay(0, 3)
    z_direct(1, 3)
    w_local.wait()
    taken(wg.at[pl.ds(0, yn), pl.ds(1, ZH - 1)], wq_r.at[0])()

    def project(c):
        at = pl.ds(c * tr, tr)
        for head in range(2):
            came(head, c, 1 - turn(c))
            az(head, c, 2).wait_recv()
        total = None
        for head in range(2):
            left = jnp.concatenate([ag[r, head, at, :] for r in range(ZH)], axis=1)
            n = wg.shape[0] // 2
            right = jnp.concatenate(
                [wg[head * n:(head + 1) * n, r].reshape(HD, slab) for r in range(ZH)], axis=0
            )
            term = jnp.dot(left, right, preferred_element_type=jnp.float32)
            total = term if total is None else total + term
        xs[c] = jnp.transpose(total).astype(jnp.bfloat16).reshape(xn, own, tr)
        for r in sorted(range(1, xn), key=lambda r: -min(r, xn - r)):
            x_copy(c, r).start()

    def x_copy(c, r):
        to = lax.rem(x_at + r, xn)
        return remote(xs.at[c, to], xr.at[c, r - 1], x_s.at[0], x_r.at[c], {"x": to})

    def mix(c):
        taken(xr.at[c], x_r.at[c])()
        total = xs[c, x_at].astype(jnp.float32)
        for r in range(1, xn):
            total = total + xr[c, r - 1].astype(jnp.float32)
        ot[c] = total.astype(jnp.bfloat16)
        pltpu.make_async_copy(ot.at[c], out_hbm.at[:, pl.ds(c * tr, tr)], o_s.at[0]).start()

    project(0)
    z_relay(1, 2)
    project(1)
    z_relay(1, 3)
    mix(0)
    project(2)
    project(3)
    mix(1)
    mix(2)
    mix(3)
    for slot in (NEAR, FAR, PARTNER, RELAY):
        where(gives[slot], marks(slot).wait_send)
        where(gives[slot], given(kv.at[slot], kv_s.at[slot]))
    given(wg.at[0], wz_s.at[0])()
    given(wg.at[pl.ds(0, 2 * yn - 1), pl.ds(1, ZH - 1)], w_s.at[0])()
    given(ag.at[pl.ds(0, 3)], az_s.at[0])()
    given(xr, x_s.at[0])()
    pltpu.make_async_copy(ot, ot, o_s.at[0]).wait()


def shards(yn, xn, queries, keys, values, segment_ids, out_weight):
    rows = queries.shape[0]
    depth, features = out_weight.shape
    own = features // (ZH * xn)
    slab = features // ZH
    wb = depth // (2 * yn)
    ids = segment_ids.reshape(1, rows)
    weight = out_weight.reshape(2 * yn, wb, features)
    dma = pltpu.SemaphoreType.DMA
    bf16, f32 = jnp.bfloat16, jnp.float32
    hbm = pl.BlockSpec(memory_space=pl.ANY)
    ups, downs = yn // 2, max(1, (yn - 1) // 2)
    out = pl.pallas_call(
        functools.partial(kernel, yn, xn),
        out_shape=jax.ShapeDtypeStruct((own, rows), bf16),
        in_specs=[hbm] * 5,
        out_specs=hbm,
        scratch_shapes=[
            pltpu.VMEM((rows, 2 * HD), bf16),
            pltpu.VMEM((5, 4, rows, HD), bf16),
            pltpu.VMEM((5, 1, rows), jnp.int32),
            pltpu.VMEM((rows, HD), f32),
            pltpu.VMEM((rows, HD), f32),
            pltpu.VMEM((rows, HD), f32),
            pltpu.VMEM((rows, HD), f32),
            pltpu.VMEM((ZH, 2, rows, HD), bf16),
            pltpu.VMEM((2 * yn, ZH, wb, slab), bf16),
            pltpu.VMEM((wb, slab), bf16),
            pltpu.VMEM((CH, xn, own, rows // CH), bf16),
            pltpu.VMEM((CH, xn - 1, own, rows // CH), bf16),
            pltpu.VMEM((CH, own, rows // CH), bf16),
            dma((4,)), dma((4, 2)), dma((4,)), dma((4,)),
            dma((1,)), dma((2,)),
            dma((1,)), dma((ups,)), dma((downs,)), dma((1,)),
            dma((1,)), dma((2, CH, 3)),
            dma((1,)), dma((CH,)),
            dma((1,)), dma((4,)),
        ],
        compiler_params=pltpu.CompilerParams(
            collective_id=0, has_side_effects=True, vmem_limit_bytes=60 * 1024 * 1024
        ),
    )(queries, keys, values, ids, weight)
    return jnp.transpose(out)


def build(mesh, yn):
    sn, hn = mesh.shape["seq"], mesh.shape["head"]
    torus = Mesh(mesh.devices.reshape(sn, ZH, hn // ZH), ("seq", "zh", "x"))
    head = ("zh", "x")
    in_specs = (P("seq", head), P("seq", head), P("seq", head), P("seq"), P(head, None))
    return jax.shard_map(
        functools.partial(shards, yn, hn // ZH),
        mesh=torus, in_specs=in_specs, out_specs=P("seq", head), check_vma=False,
    )


def solution(mesh):
    return build(mesh, Y)
```
